32 devices in a mesh: sub: 8 (over z, y), grp: 4 (over x, core).
Axes of the slice: x: 2, y: 2, z: 4, core: 2. Of those that a mesh axis runs over, the one named last changes fastest.
Arguments:
- schur: bfloat16 [64, 1024, 1024], P(('sub', 'grp')), may hold values from -6 to 45, as said below
- free_displacement: float32 [64, 32, 1024], P(('sub', 'grp')), may hold values from -200 to 200
- rigid_traces: float32 [64, 6, 1024], P(('sub', 'grp')), may hold values from -0.75 to 0.75
- rigid_load: float32 [64, 6, 32], P(('sub', 'grp')), may hold values from -48 to 48
- coarse_inverse: float32 [384, 384], P(('sub', 'grp')), may hold values from -0.1 to 0.5, as said below
- face_map: int32 [64, 4, 256], P(('sub', 'grp')), may hold values from 0 to 1024, as said below
Outputs:
- multipliers: float32 [64, 4, 32, 256], P(('sub', 'grp'))
- residual: float32 [64, 4, 32, 256], P(('sub', 'grp'))
The draws below stay inside these ranges and needn't reach their ends.
Inputs may be any that keep to these rules, and one draw needn't show every extreme that they name: `schur`: each subdomain's matrix is symmetric positive definite. `coarse_inverse`: Symmetric. `face_map`: entry w of face f of subdomain s names the interface unknown of s that multiplier slot w of that face acts on, or 1024 for an unused slot. Across a face, slot w on both sides is the same multiplier, and both sides leave it unused together; faces on the boundary of the grid are unused throughout; within one subdomain the used entries are distinct.
All inputs are finite; a program needn't handle non-finite values.
Results may differ from the reference program's by a relative error of at most 0.006.
Values sent between devices are 32-bit elements; how exact they have to be, the bound alone decides.
A program may use at most 64 MiB of HBM per device.

```python
import math
import jax
import jax.numpy as jnp
from jax import lax

IFACE = 1024
NBR = 4
MODES = 6
RHS = 32
ITERS = 2
W_PAD = 256
SLABS = 8
COLS = 8
SUBS = 64
COARSE = 384


def draw_schur(key, part):

    def one_block(block_key):
        key_noise, key_diagonal = jax.random.split(block_key, 2)
        random_noise = jnp.clip(jax.random.normal(key_noise, (IFACE, IFACE), jnp.float32), -4.0, 4.0)
        symmetric = (random_noise + random_noise.T) * (0.8 / math.sqrt(2.0 * IFACE))
        diagonal = jax.random.uniform(key_diagonal, (IFACE,), jnp.float32, 2.0, 4.0)
        matrix = symmetric + jnp.diag(diagonal)
        return matrix.astype(jnp.bfloat16)
    return lax.map(one_block, jax.random.split(key, SUBS))


def draw_coarse_inverse(key, part):
    key_noise, key_diagonal = jax.random.split(jax.random.fold_in(key, 17), 2)
    random_noise = jax.random.normal(key_noise, (COARSE, COARSE), jnp.float32)
    symmetric = (random_noise + random_noise.T) * (0.028 / math.sqrt(2.0 * COARSE))
    diagonal = jax.random.uniform(key_diagonal, (COARSE,), jnp.float32, 0.03, 0.06)
    matrix = symmetric + jnp.diag(diagonal)
    return matrix


def draw_free_displacement(key, part):
    key_base, key_columns = jax.random.split(jax.random.fold_in(key, 29), 2)
    normal_base = jax.random.normal(key_base, (SUBS, RHS, IFACE), jnp.float32)
    rising = jnp.exp(jnp.arange(SUBS, dtype=jnp.float32) * (math.log(10.0) / max(SUBS - 1, 1)) - 0.5 * math.log(10.0))
    columns = jnp.exp(jax.random.uniform(key_columns, (RHS,), jnp.float32, -0.5 * math.log(10.0), 0.5 * math.log(10.0)))
    values = normal_base * rising[:, None, None] * columns[None, :, None]
    return jnp.clip(values, -200.0, 200.0)


def interface_slots(slot_key, count, lengths):
    orderings = jax.vmap(lambda one_key: jax.random.permutation(one_key, W_PAD))(jax.random.split(slot_key, count))
    return (orderings < lengths.reshape(count, 1)).astype(jnp.int32)


def draw_face_map(key, part):
    key_list = jax.random.split(jax.random.fold_in(key, 41), 6)
    half_slots = W_PAD // 2
    x_count = (SLABS - 1) * COLS
    z_count = SLABS * (COLS - 1)
    x_lengths = jax.random.randint(key_list[0], (x_count,), half_slots, W_PAD + 1)
    full_at = jax.random.randint(key_list[1], (), 0, x_count)
    x_lengths = x_lengths.at[full_at].set(W_PAD)
    z_lengths = jax.random.randint(key_list[2], (z_count,), half_slots, W_PAD + 1)
    x_used = interface_slots(key_list[3], x_count, x_lengths).reshape(SLABS - 1, COLS, W_PAD)
    z_used = interface_slots(key_list[4], z_count, z_lengths).reshape(SLABS, COLS - 1, W_PAD)
    zero_slab = jnp.zeros((1, COLS, W_PAD), jnp.int32)
    zero_column = jnp.zeros((SLABS, 1, W_PAD), jnp.int32)
    used_slots = jnp.stack([jnp.concatenate([zero_slab, x_used], axis=0), jnp.concatenate([x_used, zero_slab], axis=0), jnp.concatenate([zero_column, z_used], axis=1), jnp.concatenate([z_used, zero_column], axis=1)], axis=2).reshape(SUBS, NBR * W_PAD)
    slot_number = jnp.cumsum(used_slots, axis=1) - 1
    orderings = jax.vmap(lambda one_key: jax.random.permutation(one_key, IFACE))(jax.random.split(key_list[5], SUBS))
    unknown = jnp.take_along_axis(orderings, jnp.clip(slot_number, 0, IFACE - 1), axis=1)
    return jnp.where(used_slots > 0, unknown, IFACE).astype(jnp.int32).reshape(SUBS, NBR, W_PAD)


def block_scale(rng, dims, shards, least, largest):
    factor_of, own = 1.0, jax.random.fold_in(rng, 6)
    for dim, blocks in shards:
        steps = jnp.exp(jax.random.uniform(jax.random.fold_in(own, dim), (blocks,), jnp.float32, least / len(shards), largest / len(shards)))
        factor_of = factor_of * jnp.repeat(steps, dims[dim] // blocks).reshape([-1 if axis == dim else 1 for axis in range(len(dims))])
    return factor_of


def bell_draw(stream_key, shape, spread, bound, shards=(), kind=jnp.bfloat16):
    values = spread * jax.random.normal(stream_key, shape, jnp.float32)
    if shards:
        values = values * block_scale(stream_key, shape, shards, -0.22, 0.18)
    return jnp.clip(values, -bound, bound).astype(kind)


def setup_inputs(seed: int = 0) -> dict:
    arg_keys = jax.random.split(jax.random.key(seed), 7)
    return {
        "schur": draw_schur(jax.random.fold_in(arg_keys[6], 71), 0),
        "free_displacement": draw_free_displacement(jax.random.fold_in(arg_keys[6], 71), 0),
        "rigid_traces": bell_draw(arg_keys[2], (SUBS, MODES, IFACE), 0.125, 0.75, ((0, 32),), jnp.float32),
        "rigid_load": bell_draw(arg_keys[3], (SUBS, MODES, RHS), 8.0, 48.0, ((0, 32),), jnp.float32),
        "coarse_inverse": draw_coarse_inverse(jax.random.fold_in(arg_keys[6], 71), 0),
        "face_map": draw_face_map(jax.random.fold_in(arg_keys[6], 71), 0),
    }


def face_signs(dtype_name):
    return jnp.array([-1.0, 1.0, -1.0, 1.0], dtype_name).reshape(4, 1, 1)


def pick_faces(local_values, face_map):
    gathered = jnp.take(local_values, face_map.reshape(-1), axis=1, mode="fill", fill_value=0)
    gathered = gathered.reshape(local_values.shape[0], face_map.shape[0], face_map.shape[1])
    return jnp.transpose(gathered, (1, 0, 2))


def spread_faces(dual_values, face_map):
    signed = dual_values * face_signs(dual_values.dtype)
    values = jnp.transpose(signed, (1, 0, 2)).reshape(dual_values.shape[1], -1)
    zero_block = jnp.zeros((dual_values.shape[1], IFACE), dual_values.dtype)
    return zero_block.at[:, face_map.reshape(-1)].add(values, mode="drop")


def jump_all(picked):
    blocks = picked.reshape(SLABS, COLS, NBR, RHS, W_PAD)
    zero_slab = jnp.zeros((1, COLS, RHS, W_PAD), picked.dtype)
    zero_column = jnp.zeros((SLABS, 1, RHS, W_PAD), picked.dtype)
    from_lower_x = jnp.concatenate([zero_slab, blocks[:-1, :, 1]], axis=0)
    from_upper_x = jnp.concatenate([blocks[1:, :, 0], zero_slab], axis=0)
    from_lower_z = jnp.concatenate([zero_column, blocks[:, :-1, 3]], axis=1)
    from_upper_z = jnp.concatenate([blocks[:, 1:, 2], zero_column], axis=1)
    received = jnp.stack([from_lower_x, from_upper_x, from_lower_z, from_upper_z], axis=2)
    return face_signs(picked.dtype) * (picked - received.reshape(picked.shape))


def inner_sum(first, second):
    return jnp.sum(first * second, axis=(0, 1, 3))


def per_load(vector):
    return vector.reshape(1, 1, -1, 1)


def schur_apply(spread_now, schur):
    return lax.map(lambda operands: jnp.dot(operands[0], operands[1], preferred_element_type=jnp.float32), (spread_now, schur))


def lift(coefficients, rigid_traces, face_map):
    lifted = jnp.einsum("smk,smi->ski", coefficients, rigid_traces, precision=lax.Precision.HIGHEST)
    return jump_all(jax.vmap(pick_faces)(lifted, face_map))


def coarse_solve(rigid_modes, coarse_inverse):
    flattened = rigid_modes.reshape(COARSE, RHS)
    solved = jnp.dot(coarse_inverse, flattened, precision=lax.Precision.HIGHEST, preferred_element_type=jnp.float32)
    return solved.reshape(SUBS, MODES, RHS)


def project(dual_values, rigid_traces, coarse_inverse, face_map):
    spread_all = jax.vmap(spread_faces)(dual_values, face_map)
    rigid_modes = jnp.einsum("smi,ski->smk", rigid_traces, spread_all, precision=lax.Precision.HIGHEST)
    return dual_values - lift(coarse_solve(rigid_modes, coarse_inverse), rigid_traces, face_map)


def reference(schur, free_displacement, rigid_traces, rigid_load, coarse_inverse, face_map):
    multipliers = lift(coarse_solve(rigid_load, coarse_inverse), rigid_traces, face_map)
    spread_now = jax.vmap(spread_faces)(multipliers, face_map).astype(jnp.bfloat16)
    product = schur_apply(spread_now, schur)
    residual = jump_all(jax.vmap(pick_faces)(free_displacement - product, face_map))
    projected = project(residual, rigid_traces, coarse_inverse, face_map)
    direction = projected
    norm_now = inner_sum(projected, projected)
    for iteration in range(ITERS):
        spread_now = jax.vmap(spread_faces)(direction, face_map).astype(jnp.bfloat16)
        product = schur_apply(spread_now, schur)
        image = jump_all(jax.vmap(pick_faces)(product, face_map))
        step_size = per_load(norm_now / inner_sum(direction, image))
        multipliers = multipliers + step_size * direction
        residual = residual - step_size * image
        if iteration + 1 < ITERS:
            projected = project(residual, rigid_traces, coarse_inverse, face_map)
            norm_next = inner_sum(projected, projected)
            direction = projected + per_load(norm_next / norm_now) * direction
            norm_now = norm_next
    return multipliers, residual
```

```python
import functools

import jax
import jax.numpy as jnp
from jax import lax
from jax.experimental import pallas as pl
from jax.experimental.pallas import tpu as pltpu
from jax.sharding import PartitionSpec as P

BF = jnp.bfloat16
F32 = jnp.float32
MESH = pl.DeviceIdType.MESH
NT = (((1,), (1,)), ((), ()))
NN = (((1,), (0,)), ((), ()))


def two(x):
    hi = x.astype(BF)
    return hi, (x - hi.astype(F32)).astype(BF)


def three(x):
    hi = x.astype(BF)
    rest = x - hi.astype(F32)
    mid = rest.astype(BF)
    return hi, mid, (rest - mid.astype(F32)).astype(BF)


def dot(a, b, dims=NN):
    return lax.dot_general(a, b, dims, preferred_element_type=F32)


def kernel(n_sub, n_grp, schur, free, traces, rigid, inverse, fmap, mult_out, res_out,
           s_buf, pt, tmat, rw, rx, kall, kn, wlift, wf, rmod, rf, mult, res, d0, w0, p1,
           z0, z1, z2, x0, x1, x2, load, kin, pay, gath,
           s_sem, ag_send, ag_recv, ag_loc, ex_send, ex_recv, kx_send, kx_recv):
    n_dev = n_sub * n_grp
    i_sub = lax.axis_index("sub")
    i_grp = lax.axis_index("grp")
    me = i_sub * n_grp + i_grp
    loads = free.shape[1]
    unk = free.shape[2]
    width = fmap.shape[2]
    nr = 4 * n_dev

    s_copy = pltpu.make_async_copy(schur, s_buf, s_sem)
    s_copy.start()

    barrier = pltpu.get_barrier_semaphore()

    def greet(r, carry):
        other = lax.rem(me + r, n_dev)
        pl.semaphore_signal(barrier, inc=1, device_id=(other // n_grp, lax.rem(other, n_grp)),
                            device_id_type=MESH)
        return carry
    lax.fori_loop(1, n_dev, greet, 0)

    for l in range(2):
        for f in range(4):
            row = fmap[l, f:f + 1, :]
            rows = lax.broadcasted_iota(jnp.int32, (unk, width), 0)
            sign = -1.0 if f in (0, 2) else 1.0
            pt[l, f] = jnp.where(rows == row, sign, 0.0).astype(BF)

    for l in range(2):
        h, m, o = three(traces[:, l, :])
        pad = jnp.zeros((2, unk), BF)
        stack = jnp.concatenate([h, pad, m, pad, o, pad], axis=0)
        for f in range(4):
            r = dot(stack, pt[l, f])
            rw[f, l] = r[0:8] + r[8:16] + r[16:24]

    low_sub = i_sub > 0
    up_sub = i_sub < n_sub - 1
    low_grp = i_grp > 0
    up_grp = i_grp < n_grp - 1
    near = (
        (up_sub, (i_sub + 1, i_grp), low_sub),
        (low_sub, (i_sub - 1, i_grp), up_sub),
        (up_grp, (i_sub, i_grp + 1), low_grp),
        (low_grp, (i_sub, i_grp - 1), up_grp),
    )
    sides = (
        (near[0], 1, 0, 0, 0),
        (near[1], 0, 0, 1, 0),
        (near[3], 2, 0, 3, 1),
        (near[0], 1, 1, 0, 1),
        (near[1], 0, 1, 1, 1),
        (near[2], 3, 1, 2, 0),
    )

    def blank(buf):
        for (_, _, come), _, _, land, l_land in sides:
            @pl.when(jnp.logical_not(come))
            def _():
                buf[land, l_land] = jnp.zeros(buf.shape[2:], F32)

    def exchange(src, buf, phase):
        copies = []
        for n, ((there, device, come), face, l_src, land, l_land) in enumerate(sides):
            copies.append((pltpu.make_async_remote_copy(
                src_ref=src.at[face, l_src], dst_ref=buf.at[land, l_land],
                send_sem=ex_send.at[phase, n], recv_sem=ex_recv.at[phase, n],
                device_id=device, device_id_type=MESH), there, come))
        return copies

    def begin(copies):
        for c, there, _ in copies:
            @pl.when(there)
            def _(c=c):
                c.start()

    def finish(copies, send):
        for c, there, come in copies:
            if send:
                @pl.when(there)
                def _(c=c):
                    c.wait_send()
            else:
                @pl.when(come)
                def _(c=c):
                    c.wait_recv()

    turn = 1 - 2 * (i_sub // (n_sub // 2))

    def gather_start(src, phase):
        own = pltpu.make_async_copy(src, gath.at[phase, me], ag_loc.at[phase])
        own.start()

        def send(n, carry):
            row = lax.rem(i_sub + turn * (n_sub - 1 - n) + n_sub, n_sub)
            for k in range(n_grp - 1, -1, -1):
                def one():
                    pltpu.make_async_remote_copy(
                        src_ref=src, dst_ref=gath.at[phase, me], send_sem=ag_send.at[phase],
                        recv_sem=ag_recv.at[phase], device_id=(row, lax.rem(i_grp + k, n_grp)),
                        device_id_type=MESH).start()
                if k == 0:
                    pl.when(n < n_sub - 1)(one)
                else:
                    one()
            return carry
        lax.fori_loop(0, n_sub, send, 0)
        return own

    def gather_finish(own, phase):
        own.wait()
        many = gath.at[phase, pl.ds(0, n_dev - 1)]
        pltpu.make_async_copy(many, many, ag_recv.at[phase]).wait()
        pltpu.make_async_copy(many, many, ag_send.at[phase]).wait()

    parts = [rigid[3 * (g % 2):3 * (g % 2) + 3, g // 2, :] for g in range(4)]
    load[...] = jnp.concatenate([jnp.concatenate(parts, axis=1), jnp.zeros((1, 128), F32)], axis=0)
    own = inverse.shape[0]
    group = 32 if n_dev % 32 == 0 else n_dev
    cols = lax.broadcasted_iota(jnp.int32, (own * group, 4 * group), 0)
    slot = lax.broadcasted_iota(jnp.int32, (own * group, 4 * group), 1)
    base = own * (slot // 4) + lax.rem(slot, 4)
    picks = [jnp.where((lax.rem(slot, 4) < 3) & (cols == base + 3 * g), 1.0, 0.0).astype(BF) for g in range(4)]
    for n in range(n_dev // group):
        pad = jnp.zeros((4, own * group), F32)
        part = jnp.concatenate([inverse[:, n * own * group:(n + 1) * own * group], pad], axis=0)
        stack = jnp.concatenate(three(part), axis=0)
        for g in range(4):
            r = dot(stack, picks[g])
            kin[g, :, n * 4 * group:(n + 1) * 4 * group] = r[0:16] + r[16:32] + r[32:48]
    blank(rx)
    blank(x0)
    blank(x1)
    blank(x2)
    for n, (_, _, come) in enumerate(near):
        @pl.when(jnp.logical_not(come))
        def _(n=n):
            kall[n + 1] = jnp.zeros(kall.shape[1:], F32)
    kall[0] = kin[...]
    g_of = lax.broadcasted_iota(jnp.int32, (4, 16, nr), 0)
    j_of = lax.broadcasted_iota(jnp.int32, (4, 16, nr), 1)
    r_of = lax.broadcasted_iota(jnp.int32, (4, 16, nr), 2)
    kall[5] = jnp.where((g_of == j_of) & (lax.rem(r_of, 4) == 3), 1.0, 0.0)
    kall[6] = jnp.zeros(kall.shape[1:], F32)
    kall[7] = jnp.zeros(kall.shape[1:], F32)

    pl.semaphore_wait(barrier, n_dev - 1)

    own_a = gather_start(load, 0)
    rcopies = exchange(rw, rx, 3)
    begin(rcopies)
    kcopies = []
    for n, (there, device, come) in enumerate(near):
        c = pltpu.make_async_remote_copy(
            src_ref=kin, dst_ref=kall.at[n + 1], send_sem=kx_send.at[n], recv_sem=kx_recv.at[n],
            device_id=device, device_id_type=MESH)
        kcopies.append((c, there, come))

        @pl.when(there)
        def _(c=c):
            c.start()

    rf[...] = jnp.zeros(rf.shape, F32)
    wf[...] = jnp.zeros(wf.shape, F32)
    for l in range(2):
        for f in range(4):
            r = rw[f, l]
            rf[l, f, 16 * l:16 * l + 3, :] = r[0:3]
            rf[l, f, 16 * l + 8:16 * l + 11, :] = r[3:6]
            wf[l, f, 6 * l:6 * l + 6, :] = r[0:6]
            h, o = two(rf[l, f])
            rmod[l, f, 0:32] = h
            rmod[l, f, 32:64] = o
    wf[0, 3, 6:12, :] = rw[2, 1, 0:6, :]
    wf[1, 2, 0:6, :] = rw[3, 0, 0:6, :]

    s_copy.wait()
    def columns(l):
        def face(f, carry):
            tmat[l, f] = dot(s_buf[l], pt[l, f]).astype(BF)
            return carry
        lax.fori_loop(0, 4, face, 0)

    def to_slots(value, l):
        stack = jnp.concatenate(three(value), axis=0)
        for f in range(4):
            r = dot(stack, pt[l, f])
            z0[f, l] = r[0:loads] + r[loads:2 * loads] + r[2 * loads:3 * loads]

    to_slots(free[0], 0)
    columns(0)

    finish(rcopies, False)
    finish(kcopies, False)
    for l in range(2):
        wf[l, 0, 16 + 6 * l:22 + 6 * l, :] = rx[0, l, 0:6, :]
        wf[l, 1, 32 + 6 * l:38 + 6 * l, :] = rx[1, l, 0:6, :]
    wf[0, 2, 54:60, :] = rx[2, 0, 0:6, :]
    wf[1, 3, 64:70, :] = rx[3, 1, 0:6, :]
    for l in range(2):
        for f in range(4):
            h, o = two(wf[l, f])
            wlift[l, f, 0:128] = h
            wlift[l, f, 128:256] = o
    for g in range(4):
        h, o = two(kall[:, g].reshape(128, nr))
        kn[0:128, g * nr:(g + 1) * nr] = h
        kn[128:256, g * nr:(g + 1) * nr] = o

    def coarse(own, phase):
        gather_finish(own, phase)
        gt = gath[phase].reshape(nr, 128).T
        x = jnp.concatenate([gt[0:32], gt[32:64], gt[64:96], gt[96:128]], axis=1)
        x = jnp.concatenate(two(x), axis=0)
        r = dot(x, kn[...], NT)
        r = r[0:32] + r[32:64]
        return r[:, 0:128] + r[:, 128:256]

    def lifted(c):
        h, o = two(c)
        return jnp.concatenate([jnp.concatenate([h, h], axis=1), jnp.concatenate([o, o], axis=1)], axis=0)

    def lift(stack, l, f):
        r = dot(stack, wlift[l, f])
        return r[0:32] + r[32:64]

    def modes(field):
        total = jnp.zeros((64, 64), F32)
        for l in range(2):
            for f in range(4):
                total += dot(rmod[l, f], jnp.concatenate(two(field[l, f]), axis=0), NT)
        total = total[0:32] + total[32:64]
        return total[:, 0:32] + total[:, 32:64]

    def rowsums(*fields):
        v = jnp.concatenate([x[:, 0:128] + x[:, 128:256] for x in fields], axis=0)
        n = v.shape[0]
        r = dot(jnp.ones((8, 128), BF), jnp.concatenate(three(v), axis=0), NT)
        r = r[:, 0:n] + r[:, n:2 * n] + r[:, 2 * n:3 * n]
        return [r[:, 32 * k:32 * k + 32] for k in range(len(fields))]

    def pack(e, dots, phase):
        row = lax.broadcasted_iota(jnp.int32, (8, 32), 0)
        parts = []
        for g in range(4):
            v = jnp.zeros((8, 32), F32) if e is None else e[8 * g:8 * g + 8]
            if g < len(dots):
                v = jnp.where(row == 3, dots[g], v)
            parts.append(v)
        pay[phase] = jnp.concatenate(parts, axis=1)[0:4]

    def spread(field, l):
        y = jnp.zeros((32, unk), F32)
        for f in range(4):
            y += dot(field[l, f].astype(BF), pt[l, f], NT)
        return y.astype(BF)

    def apply(field, put, copies):
        for l in range(2):
            y = spread(field, l)
            for f in range(4):
                put(l, f, dot(y, tmat[l, f]))
            begin(copies[3 * l:3 * l + 3])

    def jumped(z, x, l, f):
        if (l, f) == (0, 3):
            return z[3, 0] + z[2, 1]
        if (l, f) == (1, 2):
            return z[2, 1] + z[3, 0]
        return z[f, l] + x[f, l]

    both = [(l, f) for l in range(2) for f in range(4)]

    stack = lifted(coarse(own_a, 0))
    for l, f in both:
        mult[l, f] = lift(stack, l, f)

    copies0 = exchange(z0, x0, 0)
    y = spread(mult, 0)
    for f in range(4):
        z0[f, 0] = z0[f, 0] - dot(y, tmat[0, f])
    begin(copies0[0:3])
    to_slots(free[1] - dot(spread(mult, 1), s_buf[1]), 1)
    begin(copies0[3:6])
    finish(copies0, False)
    for l, f in both:
        res[l, f] = jumped(z0, x0, l, f)
    pack(modes(res), [], 1)
    own_b = gather_start(pay.at[1], 1)
    columns(1)
    stack = lifted(coarse(own_b, 1))
    norm = jnp.zeros((32, width), F32)
    for l, f in both:
        p = res[l, f] - lift(stack, l, f)
        d0[l, f] = p
        norm += p * p

    curves = []

    def put1(l, f, v):
        z1[f, l] = v
        curves.append(d0[l, f] * v)
    copies1 = exchange(z1, x1, 1)
    apply(d0, put1, copies1)
    dots = rowsums(norm, 2.0 * sum(curves[1:], curves[0]))
    finish(copies1, False)
    for l, f in both:
        w0[l, f] = jumped(z1, x1, l, f)
    pack(modes(w0), dots, 2)
    own_c = gather_start(pay.at[2], 2)
    c = coarse(own_c, 2)
    stack = lifted(c)
    norm0 = c[:, 80:81]
    curve0 = c[:, 81:82]
    step0 = norm0 / curve0
    norm = jnp.zeros((32, width), F32)
    cross = jnp.zeros((32, width), F32)
    for l, f in both:
        p = d0[l, f] - step0 * (w0[l, f] - lift(stack, l, f))
        p1[l, f] = p
        norm += p * p
        cross += p * z1[f, l]

    curves2 = []

    def put2(l, f, v):
        z2[f, l] = v
        curves2.append(p1[l, f] * v)
    apply(p1, put2, [])
    copies2 = exchange(z2, x2, 2)
    pack(None, rowsums(norm, 2.0 * sum(curves2[1:], curves2[0]), 2.0 * cross), 3)
    own_d = gather_start(pay.at[3], 3)
    begin(copies2)
    for l, f in both:
        mult[l, f] = mult[l, f] + step0 * d0[l, f]
        res[l, f] = res[l, f] - step0 * w0[l, f]
    finish(copies2, False)
    for group in (rcopies, kcopies, copies0, copies1, copies2):
        finish(group, True)
    c = coarse(own_d, 3)
    norm1 = c[:, 80:81]
    beta = norm1 / norm0
    curve1 = c[:, 81:82] + 2.0 * beta * c[:, 82:83] + beta * beta * curve0
    step1 = norm1 / curve1
    for l, f in both:
        mult_out[l, f] = mult[l, f] + step1 * (p1[l, f] + beta * d0[l, f])
        res_out[l, f] = res[l, f] - step1 * (jumped(z2, x2, l, f) + beta * w0[l, f])


def hand_over(mult, res, mult_out, res_out, sem):
    copies = [pltpu.make_async_copy(a, b, sem.at[n]) for n, (a, b) in enumerate(((mult, mult_out), (res, res_out)))]
    for c in copies:
        c.start()
    for c in copies:
        c.wait()


def local(n_sub, n_grp, schur, free, traces, load, coarse_inverse, face_map):
    n_dev = n_sub * n_grp
    loads, unk = free.shape[1], free.shape[2]
    width = face_map.shape[2]
    nr = 4 * n_dev
    vm = pl.BlockSpec(memory_space=pltpu.VMEM)
    hbm = pl.BlockSpec(memory_space=pl.ANY)
    field = pltpu.VMEM((2, 4, loads, width), F32)
    face = pltpu.VMEM((4, 2, loads, width), F32)
    dma = pltpu.SemaphoreType.DMA
    out = jax.ShapeDtypeStruct((2, 4, loads, width), F32)
    held = pltpu.VMEM((2, 4, loads, width), F32)
    results = pl.pallas_call(
        functools.partial(kernel, n_sub, n_grp),
        out_shape=(held, held),
        in_specs=[pl.BlockSpec(memory_space=pl.ANY)] + [vm] * 5,
        out_specs=(vm, vm),
        scratch_shapes=[
            pltpu.VMEM((2, unk, unk), BF),
            pltpu.VMEM((2, 4, unk, width), BF),
            pltpu.VMEM((2, 4, unk, width), BF),
            pltpu.VMEM((4, 2, 8, width), F32),
            pltpu.VMEM((4, 2, 8, width), F32),
            pltpu.VMEM((8, 4, 16, nr), F32),
            pltpu.VMEM((256, 4 * nr), BF),
            pltpu.VMEM((2, 4, 256, width), BF),
            pltpu.VMEM((2, 4, 128, width), F32),
            pltpu.VMEM((2, 4, 64, width), BF),
            pltpu.VMEM((2, 4, 32, width), F32),
            field, field, field, field, field,
            face, face, face, face, face, face,
            pltpu.VMEM((4, 128), F32),
            pltpu.VMEM((4, 16, nr), F32),
            pltpu.VMEM((4, 4, 128), F32),
            pltpu.VMEM((4, n_dev, 4, 128), F32),
            dma, dma((4,)), dma((4,)), dma((4,)), dma((4, 6)), dma((4, 6)), dma((4,)), dma((4,)),
        ],
        compiler_params=pltpu.CompilerParams(
            collective_id=0, has_side_effects=True, vmem_limit_bytes=56 * 1024 * 1024),
    )(schur, free, traces.transpose(1, 0, 2), load.transpose(1, 0, 2), coarse_inverse, face_map)
    return pl.pallas_call(
        hand_over, out_shape=(out, out), in_specs=[vm] * 2, out_specs=(hbm, hbm),
        scratch_shapes=[dma((2,))],
        compiler_params=pltpu.CompilerParams(vmem_limit_bytes=8 * 1024 * 1024))(*results)


def solution(mesh):
    both = ("sub", "grp")
    three_d = P(both, None, None)
    out = P(both, None, None, None)
    return jax.shard_map(
        functools.partial(local, mesh.shape["sub"], mesh.shape["grp"]), mesh=mesh,
        in_specs=(three_d, three_d, three_d, three_d, P(both, None), three_d),
        out_specs=(out, out), check_vma=False)
```

```python
import functools

import jax
import jax.numpy as jnp
from jax import lax
from jax.experimental import pallas as pl
from jax.experimental.pallas import tpu as pltpu
from jax.sharding import PartitionSpec as P

BF = jnp.bfloat16
F32 = jnp.float32
MESH = pl.DeviceIdType.MESH
NT = (((1,), (1,)), ((), ()))
NN = (((1,), (0,)), ((), ()))


def two(x):
    hi = x.astype(BF)
    return hi, (x - hi.astype(F32)).astype(BF)


def three(x):
    hi = x.astype(BF)
    rest = x - hi.astype(F32)
    mid = rest.astype(BF)
    return hi, mid, (rest - mid.astype(F32)).astype(BF)


def dot(a, b, dims=NN):
    return lax.dot_general(a, b, dims, preferred_element_type=F32)


def kernel(n_sub, n_grp, schur, free, traces, rigid, inverse, fmap, mult_out, res_out,
           s_buf, pt, ybuf, ysb, sgb, rw, rx, kin, kall, kn, wf, wlift, bst, tbuf, tzero, tout, tin,
           mult, res, d0, w0, p1, su, z0, z1, z2, x0, x1, x2, load, pay, gath,
           s_sem, ag_send, ag_recv, ag_loc, ex_send, ex_recv, kx_send, kx_recv, tx_send, tx_recv):
    n_dev = n_sub * n_grp
    i_sub = lax.axis_index("sub")
    i_grp = lax.axis_index("grp")
    me = i_sub * n_grp + i_grp
    loads = free.shape[1]
    unk = free.shape[2]
    width = fmap.shape[2]
    nr = 4 * n_dev
    both = [(l, f) for l in range(2) for f in range(4)]

    s_copy = pltpu.make_async_copy(schur, s_buf, s_sem)
    s_copy.start()

    barrier = pltpu.get_barrier_semaphore()

    def greet(r, carry):
        other = lax.rem(me + r, n_dev)
        pl.semaphore_signal(barrier, inc=1, device_id=(other // n_grp, lax.rem(other, n_grp)),
                            device_id_type=MESH)
        return carry
    lax.fori_loop(1, n_dev, greet, 0)

    for l, f in both:
        row = fmap[l, f:f + 1, :]
        rows = lax.broadcasted_iota(jnp.int32, (unk, width), 0)
        sign = -1.0 if f in (0, 2) else 1.0
        pt[l, f] = jnp.where(rows == row, sign, 0.0).astype(BF)

    for l in range(2):
        h, m, o = three(traces[:, l, :])
        pad = jnp.zeros((2, unk), BF)
        stack = jnp.concatenate([h, pad, m, pad, o, pad], axis=0)
        for f in range(4):
            r = dot(stack, pt[l, f])
            rw[f, l] = r[0:8] + r[8:16] + r[16:24]

    low_sub = i_sub > 0
    up_sub = i_sub < n_sub - 1
    low_grp = i_grp > 0
    up_grp = i_grp < n_grp - 1
    near = (
        (up_sub, (i_sub + 1, i_grp), low_sub),
        (low_sub, (i_sub - 1, i_grp), up_sub),
        (up_grp, (i_sub, i_grp + 1), low_grp),
        (low_grp, (i_sub, i_grp - 1), up_grp),
    )
    sides = (
        (near[0], 1, 0, 0, 0),
        (near[1], 0, 0, 1, 0),
        (near[3], 2, 0, 3, 1),
        (near[0], 1, 1, 0, 1),
        (near[1], 0, 1, 1, 1),
        (near[2], 3, 1, 2, 0),
    )

    def blank(buf):
        for (_, _, come), _, _, land, l_land in sides:
            @pl.when(jnp.logical_not(come))
            def _():
                buf[land, l_land] = jnp.zeros(buf.shape[2:], F32)

    def exchange(src, buf, phase):
        copies = []
        for n, ((there, device, come), face, l_src, land, l_land) in enumerate(sides):
            copies.append((pltpu.make_async_remote_copy(
                src_ref=src.at[face, l_src], dst_ref=buf.at[land, l_land],
                send_sem=ex_send.at[phase, n], recv_sem=ex_recv.at[phase, n],
                device_id=device, device_id_type=MESH), there, come))
        return copies

    def swap(sources, buf, send_sem, recv_sem):
        return [(pltpu.make_async_remote_copy(
            src_ref=sources[n], dst_ref=buf.at[n], send_sem=send_sem.at[n], recv_sem=recv_sem.at[n],
            device_id=device, device_id_type=MESH), there, come)
            for n, (there, device, come) in enumerate(near)]

    def begin(copies):
        for c, there, _ in copies:
            @pl.when(there)
            def _(c=c):
                c.start()

    def finish(copies, send):
        for c, there, come in copies:
            if send:
                @pl.when(there)
                def _(c=c):
                    c.wait_send()
            else:
                @pl.when(come)
                def _(c=c):
                    c.wait_recv()

    turn = 1 - 2 * (i_sub // (n_sub // 2))

    def gather_start(src, phase):
        own = pltpu.make_async_copy(src, gath.at[phase, me], ag_loc.at[phase])
        own.start()

        def send(n, carry):
            row = lax.rem(i_sub + turn * (n_sub - 1 - n) + n_sub, n_sub)
            for k in range(n_grp - 1, -1, -1):
                def one():
                    pltpu.make_async_remote_copy(
                        src_ref=src, dst_ref=gath.at[phase, me], send_sem=ag_send.at[phase],
                        recv_sem=ag_recv.at[phase], device_id=(row, lax.rem(i_grp + k, n_grp)),
                        device_id_type=MESH).start()
                if k == 0:
                    pl.when(n < n_sub - 1)(one)
                else:
                    one()
            return carry
        lax.fori_loop(0, n_sub, send, 0)
        return own

    def gather_finish(own, phase):
        own.wait()
        many = gath.at[phase, pl.ds(0, n_dev - 1)]
        pltpu.make_async_copy(many, many, ag_recv.at[phase]).wait()
        pltpu.make_async_copy(many, many, ag_send.at[phase]).wait()

    def wide(parts, last):
        return jnp.concatenate([jnp.concatenate(parts, axis=1), last], axis=0)

    no_row = jnp.zeros((1, 4 * loads), F32)
    load[...] = wide([rigid[3 * (g % 2):3 * (g % 2) + 3, g // 2, :] for g in range(4)], no_row)
    own = inverse.shape[0]
    half = own // 2
    group = 32 if n_dev % 32 == 0 else n_dev
    cols = lax.broadcasted_iota(jnp.int32, (own * group, 4 * group), 0)
    slot = lax.broadcasted_iota(jnp.int32, (own * group, 4 * group), 1)
    base = own * (slot // 4) + lax.rem(slot, 4)
    picks = [jnp.where((lax.rem(slot, 4) < 3) & (cols == base + 3 * g), 1.0, 0.0).astype(BF) for g in range(4)]
    for n in range(n_dev // group):
        pad = jnp.zeros((8 - half, own * group), F32)
        part = inverse[:, n * own * group:(n + 1) * own * group]
        part = jnp.concatenate([part[0:half], pad, part[half:own], pad], axis=0)
        stack = jnp.concatenate(three(part), axis=0)
        for g in range(4):
            r = dot(stack, picks[g])
            kin[g, :, n * 4 * group:(n + 1) * 4 * group] = r[0:16] + r[16:32] + r[32:48]
    for buf in (rx, x0, x1, x2):
        blank(buf)
    for n, (_, _, come) in enumerate(near):
        @pl.when(jnp.logical_not(come))
        def _(n=n):
            kall[n] = jnp.zeros(kall.shape[1:], F32)
            tin[0, n] = jnp.zeros(tin.shape[2:], F32)
            tin[1, n] = jnp.zeros(tin.shape[2:], F32)
    wf[...] = jnp.zeros(wf.shape, F32)
    for l, f in both:
        wf[l, f, 8 * l:8 * l + 8] = rw[f, l]
    wf[0, 3, 8:16] = rw[2, 1]
    wf[1, 2, 0:8] = rw[3, 0]

    pl.semaphore_wait(barrier, n_dev - 1)

    rcopies = exchange(rw, rx, 3)
    begin(rcopies)
    own_a = gather_start(load, 0)
    kcopies = swap([kin] * 4, kall, kx_send, kx_recv)
    begin(kcopies)

    def doubled(x):
        return jnp.concatenate(two(x), axis=0)

    def folded(r):
        n = r.shape[0] // 2
        return r[0:n] + r[n:2 * n]

    def squared(r):
        r = folded(r)
        return r[:, 0:loads] + r[:, loads:2 * loads]

    for l in range(2):
        stack = doubled(free[l])
        for f in range(4):
            z0[f, l] = folded(dot(stack, pt[l, f]))

    finish(rcopies, False)
    for l in range(2):
        wf[l, 0, 16 + 8 * l:24 + 8 * l] = rx[0, l]
        wf[l, 1, 32 + 8 * l:40 + 8 * l] = rx[1, l]
    wf[0, 2, 48:56] = rx[2, 0]
    wf[1, 3, 56:64] = rx[3, 1]
    for l, f in both:
        wlift[l, f] = doubled(wf[l, f])
    s_copy.wait()
    t_free = jnp.zeros((128, 2 * loads), F32)
    cover = jnp.zeros((128, 128), F32)
    for l in range(2):
        y = jnp.zeros((128, unk), F32)
        for f in range(4):
            y += dot(wlift[l, f], pt[l, f], NT)
        y = y.astype(BF)
        ybuf[l] = y
        t_free += dot(y, doubled(free[l]), NT)
        v = doubled(folded(dot(y, s_buf[l])))
        ysb[l] = v
        cover += dot(v, y, NT)
    bst[...] = doubled(folded(cover))
    tzero[0] = squared(t_free)

    finish(kcopies, False)
    for g in range(4):
        rows = lax.broadcasted_iota(jnp.int32, (64, nr), 0)
        lane = lax.broadcasted_iota(jnp.int32, (64, nr), 1)
        k = jnp.concatenate([kin[g], kall[0, g], kall[1, g], kall[2, g, 8:16], kall[3, g, 0:8]], axis=0)
        h, o = two(jnp.where((rows == 8 * g + 6) & (lax.rem(lane, 4) == 3), 1.0, k))
        for n, v in enumerate((h, h, o, o)):
            kn[64 * n:64 * n + 64, g * nr:(g + 1) * nr] = v

    def coarse(own, phase):
        gather_finish(own, phase)
        gt = gath[phase].reshape(nr, 128).T
        x = jnp.concatenate([gt[0:32], gt[32:64], gt[64:96], gt[96:128]], axis=1)
        r = folded(dot(doubled(x), kn[...], NT))
        return r[:, 0:128] + r[:, 128:256]

    def send_modes(stack, phase):
        tbuf[...] = tzero[phase] - squared(dot(bst[...], stack, NT))
        nil = jnp.zeros((3, loads), F32)

        def block(a, b):
            parts = []
            for n in (a, b):
                for k in range(2):
                    parts.append(nil if n is None else tbuf[8 * n + 3 * k:8 * n + 3 * k + 3, :])
            return wide(parts, no_row)
        for n, (a, b) in enumerate(((4, 5), (2, 3), (7, None), (None, 6), (0, 1))):
            tout[phase, n] = block(a, b)
        copies = swap([tout.at[phase, n] for n in range(4)], tin.at[phase], tx_send.at[phase], tx_recv.at[phase])
        begin(copies)
        return copies

    def sum_modes(copies, phase, last):
        finish(copies, False)
        t = (tout[phase, 4] + tin[phase, 0]) + (tin[phase, 1] + tin[phase, 2]) + tin[phase, 3]
        pay[phase] = wide([t[0:3]], last)
        return gather_start(pay.at[phase], phase + 1)

    def rowsums(*fields):
        v = jnp.concatenate([x[:, 0:128] + x[:, 128:256] for x in fields], axis=0)
        n = v.shape[0]
        r = dot(jnp.ones((8, 128), BF), jnp.concatenate(three(v), axis=0), NT)
        r = r[:, 0:n] + r[:, n:2 * n] + r[:, 2 * n:3 * n]
        parts = [r[0:1, loads * k:loads * k + loads] for k in range(len(fields))]
        return jnp.concatenate(parts + [jnp.zeros((1, loads), F32)] * (4 - len(fields)), axis=1)

    def through(field, l):
        y = jnp.zeros((2 * loads, unk), F32)
        for f in range(4):
            y += dot(doubled(field[l, f]), pt[l, f], NT)
        stack = doubled(folded(dot(y.astype(BF), s_buf[l])))
        for f in range(4):
            su[l, f] = folded(dot(stack, pt[l, f]))

    def jumped(z, x, l, f):
        if (l, f) == (0, 3):
            return z[3, 0] + z[2, 1]
        if (l, f) == (1, 2):
            return z[2, 1] + z[3, 0]
        return z[f, l] + x[f, l]

    stack = doubled(coarse(own_a, 0))
    modes0 = send_modes(stack, 0)
    copies0 = exchange(z0, x0, 0)
    for l in range(2):
        for f in range(4):
            sgb[l, f] = dot(ysb[l], pt[l, f]).astype(BF)
        for f in range(4):
            z0[f, l] = z0[f, l] - folded(dot(stack, sgb[l, f]))
        begin(copies0[3 * l:3 * l + 3])
    for l, f in both:
        mult[l, f] = folded(dot(stack, wlift[l, f]))
    own_b = sum_modes(modes0, 0, no_row)

    finish(copies0, False)
    t = jnp.zeros((128, 2 * loads), F32)
    for l, f in both:
        r = jumped(z0, x0, l, f)
        res[l, f] = r
        t += dot(sgb[l, f], doubled(r), NT)
    tzero[1] = squared(t)
    for l in range(2):
        through(res, l)

    stack = doubled(coarse(own_b, 1))
    modes1 = send_modes(stack, 1)
    copies1 = exchange(z1, x1, 1)
    norm = jnp.zeros((32, width), F32)
    curve = jnp.zeros((32, width), F32)
    for l in range(2):
        for f in range(4):
            z = su[l, f] - folded(dot(stack, sgb[l, f]))
            z1[f, l] = z
            p = res[l, f] - folded(dot(stack, wlift[l, f]))
            d0[l, f] = p
            norm += p * p
            curve += p * z
        begin(copies1[3 * l:3 * l + 3])
    own_c = sum_modes(modes1, 1, rowsums(norm, 2.0 * curve))

    finish(copies1, False)
    for l, f in both:
        w0[l, f] = jumped(z1, x1, l, f)
    for l in range(2):
        through(w0, l)

    c = coarse(own_c, 2)
    stack = doubled(c)
    norm0 = c[:, 6:7]
    curve0 = c[:, 14:15]
    step0 = norm0 / curve0
    norm = jnp.zeros((32, width), F32)
    curve = jnp.zeros((32, width), F32)
    cross = jnp.zeros((32, width), F32)
    for l, f in both:
        p = d0[l, f] - step0 * (w0[l, f] - folded(dot(stack, wlift[l, f])))
        z = z1[f, l] - step0 * (su[l, f] - folded(dot(stack, sgb[l, f])))
        p1[l, f] = p
        z2[f, l] = z
        norm += p * p
        curve += p * z
        cross += p * z1[f, l]
    pay[2] = wide([jnp.zeros((3, 4 * loads), F32)], rowsums(norm, 2.0 * curve, 2.0 * cross))
    own_d = gather_start(pay.at[2], 3)
    copies2 = exchange(z2, x2, 2)
    begin(copies2)
    for l, f in both:
        mult[l, f] = mult[l, f] + step0 * d0[l, f]
        res[l, f] = res[l, f] - step0 * w0[l, f]
    finish(copies2, False)
    for group in (rcopies, kcopies, modes0, modes1, copies0, copies1, copies2):
        finish(group, True)
    c = coarse(own_d, 3)
    norm1 = c[:, 6:7]
    beta = norm1 / norm0
    curve1 = c[:, 14:15] + 2.0 * beta * c[:, 22:23] + beta * beta * curve0
    step1 = norm1 / curve1
    for l, f in both:
        mult_out[l, f] = mult[l, f] + step1 * (p1[l, f] + beta * d0[l, f])
        res_out[l, f] = res[l, f] - step1 * (jumped(z2, x2, l, f) + beta * w0[l, f])


def hand_over(mult, res, mult_out, res_out, sem):
    copies = [pltpu.make_async_copy(a, b, sem.at[n]) for n, (a, b) in enumerate(((mult, mult_out), (res, res_out)))]
    for c in copies:
        c.start()
    for c in copies:
        c.wait()


def local(n_sub, n_grp, schur, free, traces, load, coarse_inverse, face_map):
    n_dev = n_sub * n_grp
    loads, unk = free.shape[1], free.shape[2]
    width = face_map.shape[2]
    nr = 4 * n_dev
    vm = pl.BlockSpec(memory_space=pltpu.VMEM)
    hbm = pl.BlockSpec(memory_space=pl.ANY)
    field = pltpu.VMEM((2, 4, loads, width), F32)
    face = pltpu.VMEM((4, 2, loads, width), F32)
    dma = pltpu.SemaphoreType.DMA
    out = jax.ShapeDtypeStruct((2, 4, loads, width), F32)
    held = pltpu.VMEM((2, 4, loads, width), F32)
    results = pl.pallas_call(
        functools.partial(kernel, n_sub, n_grp),
        out_shape=(held, held),
        in_specs=[pl.BlockSpec(memory_space=pl.ANY)] + [vm] * 5,
        out_specs=(vm, vm),
        scratch_shapes=[
            pltpu.VMEM((2, unk, unk), BF),
            pltpu.VMEM((2, 4, unk, width), BF),
            pltpu.VMEM((2, 128, unk), BF),
            pltpu.VMEM((2, 128, unk), BF),
            pltpu.VMEM((2, 4, 128, width), BF),
            pltpu.VMEM((4, 2, 8, width), F32),
            pltpu.VMEM((4, 2, 8, width), F32),
            pltpu.VMEM((4, 16, nr), F32),
            pltpu.VMEM((4, 4, 16, nr), F32),
            pltpu.VMEM((256, 4 * nr), BF),
            pltpu.VMEM((2, 4, 64, width), F32),
            pltpu.VMEM((2, 4, 128, width), BF),
            pltpu.VMEM((128, 128), BF),
            pltpu.VMEM((64, loads), F32),
            pltpu.VMEM((2, 64, loads), F32),
            pltpu.VMEM((2, 5, 4, 4 * loads), F32),
            pltpu.VMEM((2, 4, 4, 4 * loads), F32),
            field, field, field, field, field, field,
            face, face, face, face, face, face,
            pltpu.VMEM((4, 4 * loads), F32),
            pltpu.VMEM((3, 4, 4 * loads), F32),
            pltpu.VMEM((4, n_dev, 4, 4 * loads), F32),
            dma, dma((4,)), dma((4,)), dma((4,)), dma((4, 6)), dma((4, 6)), dma((4,)), dma((4,)),
            dma((2, 4)), dma((2, 4)),
        ],
        compiler_params=pltpu.CompilerParams(
            collective_id=0, has_side_effects=True, vmem_limit_bytes=56 * 1024 * 1024),
    )(schur, free, traces.transpose(1, 0, 2), load.transpose(1, 0, 2), coarse_inverse, face_map)
    return pl.pallas_call(
        hand_over, out_shape=(out, out), in_specs=[vm] * 2, out_specs=(hbm, hbm),
        scratch_shapes=[dma((2,))],
        compiler_params=pltpu.CompilerParams(vmem_limit_bytes=8 * 1024 * 1024))(*results)


def solution(mesh):
    both = ("sub", "grp")
    three_d = P(both, None, None)
    out = P(both, None, None, None)
    return jax.shard_map(
        functools.partial(local, mesh.shape["sub"], mesh.shape["grp"]), mesh=mesh,
        in_specs=(three_d, three_d, three_d, three_d, P(both, None), three_d),
        out_specs=(out, out), check_vma=False)
```

```python
import functools

import jax
import jax.numpy as jnp
from jax import lax
from jax.experimental import pallas as pl
from jax.experimental.pallas import tpu as pltpu
from jax.sharding import PartitionSpec as P

BF = jnp.bfloat16
F32 = jnp.float32
MESH = pl.DeviceIdType.MESH
NT = (((1,), (1,)), ((), ()))
NN = (((1,), (0,)), ((), ()))


def two(x):
    hi = x.astype(BF)
    return hi, (x - hi.astype(F32)).astype(BF)


def three(x):
    hi = x.astype(BF)
    rest = x - hi.astype(F32)
    mid = rest.astype(BF)
    return hi, mid, (rest - mid.astype(F32)).astype(BF)


def dot(a, b, dims=NN):
    return lax.dot_general(a, b, dims, preferred_element_type=F32)


def kernel(n_sub, n_grp, schur, free_in, traces_in, rigid_in, inverse_in, fmap_in, mult_out, res_out,
           free, traces, rigid, inverse, fmap, s_buf, pt, ptt, ybuf, ysb, sgb, rw, rx, kin, kall, kn, wf, wlift, bst, tbuf, tzero, tout, tin,
           mult, res, d0, w0, p1, su, z0, z1, z2, x0, x1, x2, load, pay, gath,
           s_sem, in_sem, ag_send, ag_recv, ag_loc, ex_send, ex_recv, kx_send, kx_recv, tx_send, tx_recv):
    n_dev = n_sub * n_grp
    i_sub = lax.axis_index("sub")
    i_grp = lax.axis_index("grp")
    me = i_sub * n_grp + i_grp
    loads = free.shape[1]
    unk = free.shape[2]
    width = fmap.shape[2]
    nr = 4 * n_dev
    both = [(l, f) for l in range(2) for f in range(4)]

    pairs = ((fmap_in, fmap), (traces_in, traces), (rigid_in, rigid), (inverse_in, inverse), (free_in, free))
    fetch = [pltpu.make_async_copy(a, b, in_sem.at[n]) for n, (a, b) in enumerate(pairs)]
    for copy in fetch:
        copy.start()
    s_copy = pltpu.make_async_copy(schur, s_buf, s_sem)
    s_copy.start()

    barrier = pltpu.get_barrier_semaphore()

    def greet(r, carry):
        other = lax.rem(me + r, n_dev)
        pl.semaphore_signal(barrier, inc=1, device_id=(other // n_grp, lax.rem(other, n_grp)),
                            device_id_type=MESH)
        return carry
    lax.fori_loop(1, n_dev, greet, 0)

    fetch[0].wait()
    for l, f in both:
        row = fmap[l, f:f + 1, :]
        rows = lax.broadcasted_iota(jnp.int32, (unk, width), 0)
        sign = -1.0 if f in (0, 2) else 1.0
        pt[l, f] = jnp.where(rows == row, sign, 0.0).astype(BF)

    fetch[1].wait()
    for l in range(2):
        h, m, o = three(traces[:, l, :])
        pad = jnp.zeros((2, unk), BF)
        stack = jnp.concatenate([h, pad, m, pad, o, pad], axis=0)
        for f in range(4):
            r = dot(stack, pt[l, f])
            rw[f, l] = r[0:8] + r[8:16] + r[16:24]

    low_sub = i_sub > 0
    up_sub = i_sub < n_sub - 1
    low_grp = i_grp > 0
    up_grp = i_grp < n_grp - 1
    near = (
        (up_sub, (i_sub + 1, i_grp), low_sub),
        (low_sub, (i_sub - 1, i_grp), up_sub),
        (up_grp, (i_sub, i_grp + 1), low_grp),
        (low_grp, (i_sub, i_grp - 1), up_grp),
    )
    sides = (
        (near[0], 1, 0, 0, 0),
        (near[1], 0, 0, 1, 0),
        (near[3], 2, 0, 3, 1),
        (near[0], 1, 1, 0, 1),
        (near[1], 0, 1, 1, 1),
        (near[2], 3, 1, 2, 0),
    )

    def blank(buf):
        for (_, _, come), _, _, land, l_land in sides:
            @pl.when(jnp.logical_not(come))
            def _():
                buf[land, l_land] = jnp.zeros(buf.shape[2:], F32)

    def exchange(src, buf, phase):
        copies = []
        for n, ((there, device, come), face, l_src, land, l_land) in enumerate(sides):
            copies.append((pltpu.make_async_remote_copy(
                src_ref=src.at[face, l_src], dst_ref=buf.at[land, l_land],
                send_sem=ex_send.at[phase, n], recv_sem=ex_recv.at[phase, n],
                device_id=device, device_id_type=MESH), there, come))
        return copies

    def swap(sources, buf, send_sem, recv_sem):
        return [(pltpu.make_async_remote_copy(
            src_ref=sources[n], dst_ref=buf.at[n], send_sem=send_sem.at[n], recv_sem=recv_sem.at[n],
            device_id=device, device_id_type=MESH), there, come)
            for n, (there, device, come) in enumerate(near)]

    def begin(copies):
        for c, there, _ in copies:
            @pl.when(there)
            def _(c=c):
                c.start()

    def finish(copies, send):
        for c, there, come in copies:
            if send:
                @pl.when(there)
                def _(c=c):
                    c.wait_send()
            else:
                @pl.when(come)
                def _(c=c):
                    c.wait_recv()

    turn = 1 - 2 * (i_sub // (n_sub // 2))

    def gather_start(src, phase):
        own = pltpu.make_async_copy(src, gath.at[phase, me], ag_loc.at[phase])
        own.start()

        def send(n, carry):
            row = lax.rem(i_sub + turn * (n_sub - 1 - n) + n_sub, n_sub)
            for k in range(n_grp - 1, -1, -1):
                def one():
                    pltpu.make_async_remote_copy(
                        src_ref=src, dst_ref=gath.at[phase, me], send_sem=ag_send.at[phase],
                        recv_sem=ag_recv.at[phase], device_id=(row, lax.rem(i_grp + k, n_grp)),
                        device_id_type=MESH).start()
                if k == 0:
                    pl.when(n < n_sub - 1)(one)
                else:
                    one()
            return carry
        lax.fori_loop(0, n_sub, send, 0)
        return own

    def gather_finish(own, phase):
        own.wait()
        many = gath.at[phase, pl.ds(0, n_dev - 1)]
        pltpu.make_async_copy(many, many, ag_recv.at[phase]).wait()
        pltpu.make_async_copy(many, many, ag_send.at[phase]).wait()

    def wide(parts, last):
        return jnp.concatenate([jnp.concatenate(parts, axis=1), last], axis=0)

    no_row = jnp.zeros((1, 4 * loads), F32)
    fetch[2].wait()
    load[...] = wide([rigid[3 * (g % 2):3 * (g % 2) + 3, g // 2, :] for g in range(4)], no_row)
    for buf in (rx, x0, x1, x2):
        blank(buf)
    for n, (_, _, come) in enumerate(near):
        @pl.when(jnp.logical_not(come))
        def _(n=n):
            kall[n] = jnp.zeros(kall.shape[1:], F32)
            tin[0, n] = jnp.zeros(tin.shape[2:], F32)
            tin[1, n] = jnp.zeros(tin.shape[2:], F32)
    wf[...] = jnp.zeros(wf.shape, F32)
    for l, f in both:
        wf[l, f, 8 * l:8 * l + 8] = rw[f, l]
    wf[0, 3, 8:16] = rw[2, 1]
    wf[1, 2, 0:8] = rw[3, 0]

    pl.semaphore_wait(barrier, n_dev - 1)

    rcopies = exchange(rw, rx, 3)
    begin(rcopies)
    own_a = gather_start(load, 0)
    fetch[3].wait()
    own = inverse.shape[0]
    half = own // 2
    group = 32 if n_dev % 32 == 0 else n_dev
    cols = lax.broadcasted_iota(jnp.int32, (own * group, 4 * group), 0)
    slot = lax.broadcasted_iota(jnp.int32, (own * group, 4 * group), 1)
    base = own * (slot // 4) + lax.rem(slot, 4)
    picks = [jnp.where((lax.rem(slot, 4) < 3) & (cols == base + 3 * g), 1.0, 0.0).astype(BF) for g in range(4)]
    for n in range(n_dev // group):
        pad = jnp.zeros((8 - half, own * group), F32)
        part = inverse[:, n * own * group:(n + 1) * own * group]
        part = jnp.concatenate([part[0:half], pad, part[half:own], pad], axis=0)
        stack = jnp.concatenate(three(part), axis=0)
        for g in range(4):
            r = dot(stack, picks[g])
            kin[g, :, n * 4 * group:(n + 1) * 4 * group] = r[0:16] + r[16:32] + r[32:48]
    kcopies = swap([kin] * 4, kall, kx_send, kx_recv)
    begin(kcopies)

    def doubled(x):
        return jnp.concatenate(two(x), axis=0)

    def folded(r):
        n = r.shape[0] // 2
        return r[0:n] + r[n:2 * n]

    def squared(r):
        r = folded(r)
        return r[:, 0:loads] + r[:, loads:2 * loads]

    index = jnp.concatenate([fmap[0], fmap[1]], axis=0).astype(F32).T.astype(jnp.int32)
    for l, f in both:
        lane = lax.broadcasted_iota(jnp.int32, (width, unk), 1)
        sign = -1.0 if f in (0, 2) else 1.0
        ptt[l, width * f:width * f + width] = jnp.where(
            lane == index[:, 4 * l + f:4 * l + f + 1], sign, 0.0).astype(BF)

    fetch[4].wait()
    for l in range(2):
        stack = doubled(free[l])
        for f in range(4):
            z0[f, l] = folded(dot(stack, pt[l, f]))

    finish(rcopies, False)
    for l in range(2):
        wf[l, 0, 16 + 8 * l:24 + 8 * l] = rx[0, l]
        wf[l, 1, 32 + 8 * l:40 + 8 * l] = rx[1, l]
    wf[0, 2, 48:56] = rx[2, 0]
    wf[1, 3, 56:64] = rx[3, 1]
    for l, f in both:
        wlift[l, f] = doubled(wf[l, f])
    s_copy.wait()
    t_free = jnp.zeros((128, 2 * loads), F32)
    cover = jnp.zeros((128, 128), F32)
    for l in range(2):
        y = dot(jnp.concatenate([wlift[l, f] for f in range(4)], axis=1), ptt[l]).astype(BF)
        ybuf[l] = y
        t_free += dot(y, doubled(free[l]), NT)
        v = doubled(folded(dot(y, s_buf[l])))
        ysb[l] = v
        cover += dot(v, y, NT)
    bst[...] = doubled(folded(cover))
    tzero[0] = squared(t_free)

    finish(kcopies, False)
    for g in range(4):
        rows = lax.broadcasted_iota(jnp.int32, (64, nr), 0)
        lane = lax.broadcasted_iota(jnp.int32, (64, nr), 1)
        k = jnp.concatenate([kin[g], kall[0, g], kall[1, g], kall[2, g, 8:16], kall[3, g, 0:8]], axis=0)
        h, o = two(jnp.where((rows == 8 * g + 6) & (lax.rem(lane, 4) == 3), 1.0, k))
        for n, v in enumerate((h, h, o, o)):
            kn[64 * n:64 * n + 64, g * nr:(g + 1) * nr] = v

    def coarse(own, phase):
        gather_finish(own, phase)
        gt = gath[phase].reshape(nr, 128).T
        x = jnp.concatenate([gt[0:32], gt[32:64], gt[64:96], gt[96:128]], axis=1)
        r = folded(dot(doubled(x), kn[...], NT))
        return r[:, 0:128] + r[:, 128:256]

    def send_modes(stack, phase):
        tbuf[...] = tzero[phase] - squared(dot(bst[...], stack, NT))
        nil = jnp.zeros((3, loads), F32)

        def block(a, b):
            parts = []
            for n in (a, b):
                for k in range(2):
                    parts.append(nil if n is None else tbuf[8 * n + 3 * k:8 * n + 3 * k + 3, :])
            return wide(parts, no_row)
        for n, (a, b) in enumerate(((4, 5), (2, 3), (7, None), (None, 6), (0, 1))):
            tout[phase, n] = block(a, b)
        copies = swap([tout.at[phase, n] for n in range(4)], tin.at[phase], tx_send.at[phase], tx_recv.at[phase])
        begin(copies)
        return copies

    def sum_modes(copies, phase, last):
        finish(copies, False)
        t = (tout[phase, 4] + tin[phase, 0]) + (tin[phase, 1] + tin[phase, 2]) + tin[phase, 3]
        pay[phase] = wide([t[0:3]], last)
        return gather_start(pay.at[phase], phase + 1)

    def rowsums(*fields):
        v = jnp.concatenate([x[:, 0:128] + x[:, 128:256] for x in fields], axis=0)
        n = v.shape[0]
        r = dot(jnp.ones((8, 128), BF), jnp.concatenate(three(v), axis=0), NT)
        r = r[:, 0:n] + r[:, n:2 * n] + r[:, 2 * n:3 * n]
        parts = [r[0:1, loads * k:loads * k + loads] for k in range(len(fields))]
        return jnp.concatenate(parts + [jnp.zeros((1, loads), F32)] * (4 - len(fields)), axis=1)

    def through(field, l):
        y = dot(jnp.concatenate([doubled(field[l, f]) for f in range(4)], axis=1), ptt[l])
        stack = doubled(folded(dot(y.astype(BF), s_buf[l])))
        for f in range(4):
            su[l, f] = folded(dot(stack, pt[l, f]))

    def jumped(z, x, l, f):
        if (l, f) == (0, 3):
            return z[3, 0] + z[2, 1]
        if (l, f) == (1, 2):
            return z[2, 1] + z[3, 0]
        return z[f, l] + x[f, l]

    stack = doubled(coarse(own_a, 0))
    modes0 = send_modes(stack, 0)
    copies0 = exchange(z0, x0, 0)
    for l in range(2):
        for f in range(4):
            sgb[l, f] = dot(ysb[l], pt[l, f]).astype(BF)
        for f in range(4):
            z0[f, l] = z0[f, l] - folded(dot(stack, sgb[l, f]))
        begin(copies0[3 * l:3 * l + 3])
    for l, f in both:
        mult[l, f] = folded(dot(stack, wlift[l, f]))
    own_b = sum_modes(modes0, 0, no_row)

    finish(copies0, False)
    t = jnp.zeros((128, 2 * loads), F32)
    for l, f in both:
        r = jumped(z0, x0, l, f)
        res[l, f] = r
        t += dot(sgb[l, f], doubled(r), NT)
    tzero[1] = squared(t)
    through(res, 0)

    stack = doubled(coarse(own_b, 1))
    modes1 = send_modes(stack, 1)
    copies1 = exchange(z1, x1, 1)
    norm = jnp.zeros((32, width), F32)
    curve = jnp.zeros((32, width), F32)
    for l in range(2):
        if l == 1:
            through(res, 1)
        for f in range(4):
            z = su[l, f] - folded(dot(stack, sgb[l, f]))
            z1[f, l] = z
            p = res[l, f] - folded(dot(stack, wlift[l, f]))
            d0[l, f] = p
            norm += p * p
            curve += p * z
        begin(copies1[3 * l:3 * l + 3])
    own_c = sum_modes(modes1, 1, rowsums(norm, 2.0 * curve))

    finish(copies1, False)
    for l, f in both:
        w0[l, f] = jumped(z1, x1, l, f)
    for l in range(2):
        through(w0, l)

    c = coarse(own_c, 2)
    stack = doubled(c)
    norm0 = c[:, 6:7]
    curve0 = c[:, 14:15]
    step0 = norm0 / curve0
    norm = jnp.zeros((32, width), F32)
    curve = jnp.zeros((32, width), F32)
    cross = jnp.zeros((32, width), F32)
    copies2 = exchange(z2, x2, 2)
    for l, f in both:
        p = d0[l, f] - step0 * (w0[l, f] - folded(dot(stack, wlift[l, f])))
        z = z1[f, l] - step0 * (su[l, f] - folded(dot(stack, sgb[l, f])))
        p1[l, f] = p
        z2[f, l] = z
        norm += p * p
        curve += p * z
        cross += p * z1[f, l]
    pay[2] = wide([jnp.zeros((3, 4 * loads), F32)], rowsums(norm, 2.0 * curve, 2.0 * cross))
    own_d = gather_start(pay.at[2], 3)
    begin(copies2)
    for l, f in both:
        mult[l, f] = mult[l, f] + step0 * d0[l, f]
        res[l, f] = res[l, f] - step0 * w0[l, f]
    finish(copies2, False)
    for group in (rcopies, kcopies, modes0, modes1, copies0, copies1, copies2):
        finish(group, True)
    c = coarse(own_d, 3)
    norm1 = c[:, 6:7]
    beta = norm1 / norm0
    curve1 = c[:, 14:15] + 2.0 * beta * c[:, 22:23] + beta * beta * curve0
    step1 = norm1 / curve1
    for l, f in both:
        mult_out[l, f] = mult[l, f] + step1 * (p1[l, f] + beta * d0[l, f])
        res_out[l, f] = res[l, f] - step1 * (jumped(z2, x2, l, f) + beta * w0[l, f])


def hand_over(mult, res, mult_out, res_out, sem):
    copies = [pltpu.make_async_copy(a, b, sem.at[n]) for n, (a, b) in enumerate(((mult, mult_out), (res, res_out)))]
    for c in copies:
        c.start()
    for c in copies:
        c.wait()


def local(n_sub, n_grp, schur, free, traces, load, coarse_inverse, face_map):
    n_dev = n_sub * n_grp
    loads, unk = free.shape[1], free.shape[2]
    width = face_map.shape[2]
    nr = 4 * n_dev
    vm = pl.BlockSpec(memory_space=pltpu.VMEM)
    hbm = pl.BlockSpec(memory_space=pl.ANY)
    field = pltpu.VMEM((2, 4, loads, width), F32)
    face = pltpu.VMEM((4, 2, loads, width), F32)
    dma = pltpu.SemaphoreType.DMA
    out = jax.ShapeDtypeStruct((2, 4, loads, width), F32)
    held = pltpu.VMEM((2, 4, loads, width), F32)
    results = pl.pallas_call(
        functools.partial(kernel, n_sub, n_grp),
        out_shape=(held, held),
        in_specs=[hbm] * 6,
        out_specs=(vm, vm),
        scratch_shapes=[
            pltpu.VMEM(free.shape, F32),
            pltpu.VMEM((traces.shape[1], 2, unk), F32),
            pltpu.VMEM((load.shape[1], 2, loads), F32),
            pltpu.VMEM(coarse_inverse.shape, F32),
            pltpu.VMEM(face_map.shape, jnp.int32),
            pltpu.VMEM((2, unk, unk), BF),
            pltpu.VMEM((2, 4, unk, width), BF),
            pltpu.VMEM((2, 4 * width, unk), BF),
            pltpu.VMEM((2, 128, unk), BF),
            pltpu.VMEM((2, 128, unk), BF),
            pltpu.VMEM((2, 4, 128, width), BF),
            pltpu.VMEM((4, 2, 8, width), F32),
            pltpu.VMEM((4, 2, 8, width), F32),
            pltpu.VMEM((4, 16, nr), F32),
            pltpu.VMEM((4, 4, 16, nr), F32),
            pltpu.VMEM((256, 4 * nr), BF),
            pltpu.VMEM((2, 4, 64, width), F32),
            pltpu.VMEM((2, 4, 128, width), BF),
            pltpu.VMEM((128, 128), BF),
            pltpu.VMEM((64, loads), F32),
            pltpu.VMEM((2, 64, loads), F32),
            pltpu.VMEM((2, 5, 4, 4 * loads), F32),
            pltpu.VMEM((2, 4, 4, 4 * loads), F32),
            field, field, field, field, field, field,
            face, face, face, face, face, face,
            pltpu.VMEM((4, 4 * loads), F32),
            pltpu.VMEM((3, 4, 4 * loads), F32),
            pltpu.VMEM((4, n_dev, 4, 4 * loads), F32),
            dma, dma((5,)), dma((4,)), dma((4,)), dma((4,)), dma((4, 6)), dma((4, 6)), dma((4,)), dma((4,)),
            dma((2, 4)), dma((2, 4)),
        ],
        compiler_params=pltpu.CompilerParams(
            collective_id=0, has_side_effects=True, vmem_limit_bytes=56 * 1024 * 1024),
    )(schur, free, traces.transpose(1, 0, 2), load.transpose(1, 0, 2), coarse_inverse, face_map)
    return pl.pallas_call(
        hand_over, out_shape=(out, out), in_specs=[vm] * 2, out_specs=(hbm, hbm),
        scratch_shapes=[dma((2,))],
        compiler_params=pltpu.CompilerParams(vmem_limit_bytes=8 * 1024 * 1024))(*results)


def solution(mesh):
    both = ("sub", "grp")
    three_d = P(both, None, None)
    out = P(both, None, None, None)
    return jax.shard_map(
        functools.partial(local, mesh.shape["sub"], mesh.shape["grp"]), mesh=mesh,
        in_specs=(three_d, three_d, three_d, three_d, P(both, None), three_d),
        out_specs=(out, out), check_vma=False)
```

```python
import functools

import jax
import jax.numpy as jnp
from jax import lax
from jax.experimental import pallas as pl
from jax.experimental.pallas import tpu as pltpu
from jax.sharding import PartitionSpec as P

BF = jnp.bfloat16
F32 = jnp.float32
MESH = pl.DeviceIdType.MESH
NT = (((1,), (1,)), ((), ()))
NN = (((1,), (0,)), ((), ()))


def two(x):
    hi = x.astype(BF)
    return hi, (x - hi.astype(F32)).astype(BF)


def three(x):
    hi = x.astype(BF)
    rest = x - hi.astype(F32)
    mid = rest.astype(BF)
    return hi, mid, (rest - mid.astype(F32)).astype(BF)


def dot(a, b, dims=NN):
    return lax.dot_general(a, b, dims, preferred_element_type=F32)


def kernel(n_sub, n_grp, schur, free_in, traces_in, rigid_in, inverse_in, fmap_in, mult_out, res_out,
           free, traces, rigid, inverse, fmap, s_buf, pt, ptt, ybuf, ysb, sgb, rw, rx, kin, kall, kn, wf, wlift, bst, tbuf, tzero, tout, tin,
           mult, res, d0, w0, p1, su, z0, z1, z2, x0, x1, x2, load, pay, gath,
           s_sem, in_sem, ag_send, ag_recv, ag_loc, ex_send, ex_recv, kx_send, kx_recv, tx_send, tx_recv):
    n_dev = n_sub * n_grp
    i_sub = lax.axis_index("sub")
    i_grp = lax.axis_index("grp")
    me = i_sub * n_grp + i_grp
    loads = free.shape[1]
    unk = free.shape[2]
    width = fmap.shape[2]
    nr = 4 * n_dev
    both = [(l, f) for l in range(2) for f in range(4)]

    pairs = ((fmap_in, fmap), (traces_in, traces), (rigid_in, rigid), (inverse_in, inverse), (free_in, free))
    fetch = [pltpu.make_async_copy(a, b, in_sem.at[n]) for n, (a, b) in enumerate(pairs)]
    for copy in fetch:
        copy.start()
    s_copy = pltpu.make_async_copy(schur, s_buf, s_sem)
    s_copy.start()

    barrier = pltpu.get_barrier_semaphore()

    def greet(r, carry):
        other = lax.rem(me + r, n_dev)
        pl.semaphore_signal(barrier, inc=1, device_id=(other // n_grp, lax.rem(other, n_grp)),
                            device_id_type=MESH)
        return carry
    lax.fori_loop(1, n_dev, greet, 0)

    fetch[0].wait()
    for l, f in both:
        row = fmap[l, f:f + 1, :]
        rows = lax.broadcasted_iota(jnp.int32, (unk, width), 0)
        sign = -1.0 if f in (0, 2) else 1.0
        pt[l, f] = jnp.where(rows == row, sign, 0.0).astype(BF)

    fetch[1].wait()
    for l in range(2):
        h, m, o = three(traces[:, l, :])
        pad = jnp.zeros((2, unk), BF)
        stack = jnp.concatenate([h, pad, m, pad, o, pad], axis=0)
        for f in range(4):
            r = dot(stack, pt[l, f])
            rw[f, l] = r[0:8] + r[8:16] + r[16:24]

    low_sub = i_sub > 0
    up_sub = i_sub < n_sub - 1
    low_grp = i_grp > 0
    up_grp = i_grp < n_grp - 1
    near = (
        (up_sub, (i_sub + 1, i_grp), low_sub),
        (low_sub, (i_sub - 1, i_grp), up_sub),
        (up_grp, (i_sub, i_grp + 1), low_grp),
        (low_grp, (i_sub, i_grp - 1), up_grp),
    )
    sides = (
        (near[0], 1, 0, 0, 0),
        (near[1], 0, 0, 1, 0),
        (near[3], 2, 0, 3, 1),
        (near[0], 1, 1, 0, 1),
        (near[1], 0, 1, 1, 1),
        (near[2], 3, 1, 2, 0),
    )

    def blank(buf):
        for (_, _, come), _, _, land, l_land in sides:
            @pl.when(jnp.logical_not(come))
            def _():
                buf[land, l_land] = jnp.zeros(buf.shape[2:], F32)

    def exchange(src, buf, phase):
        copies = []
        for n, ((there, device, come), face, l_src, land, l_land) in enumerate(sides):
            copies.append((pltpu.make_async_remote_copy(
                src_ref=src.at[face, l_src], dst_ref=buf.at[land, l_land],
                send_sem=ex_send.at[phase, n], recv_sem=ex_recv.at[phase, n],
                device_id=device, device_id_type=MESH), there, come))
        return copies

    def swap(sources, buf, send_sem, recv_sem):
        return [(pltpu.make_async_remote_copy(
            src_ref=sources[n], dst_ref=buf.at[n], send_sem=send_sem.at[n], recv_sem=recv_sem.at[n],
            device_id=device, device_id_type=MESH), there, come)
            for n, (there, device, come) in enumerate(near)]

    def begin(copies):
        for c, there, _ in copies:
            @pl.when(there)
            def _(c=c):
                c.start()

    def finish(copies, send):
        for c, there, come in copies:
            if send:
                @pl.when(there)
                def _(c=c):
                    c.wait_send()
            else:
                @pl.when(come)
                def _(c=c):
                    c.wait_recv()

    turn = 1 - 2 * (i_sub // (n_sub // 2))

    def gather_start(src, phase):
        own = pltpu.make_async_copy(src, gath.at[phase, me], ag_loc.at[phase])
        own.start()

        def send(n, carry):
            row = lax.rem(i_sub + turn * (n_sub - 1 - n) + n_sub, n_sub)
            for k in range(n_grp - 1, -1, -1):
                def one():
                    pltpu.make_async_remote_copy(
                        src_ref=src, dst_ref=gath.at[phase, me], send_sem=ag_send.at[phase],
                        recv_sem=ag_recv.at[phase], device_id=(row, lax.rem(i_grp + k, n_grp)),
                        device_id_type=MESH).start()
                if k == 0:
                    pl.when(n < n_sub - 1)(one)
                else:
                    one()
            return carry
        lax.fori_loop(0, n_sub, send, 0)
        return own

    def gather_finish(own, phase):
        own.wait()
        many = gath.at[phase, pl.ds(0, n_dev - 1)]
        pltpu.make_async_copy(many, many, ag_recv.at[phase]).wait()

    def wide(parts, last):
        return jnp.concatenate([jnp.concatenate(parts, axis=1), last], axis=0)

    no_row = jnp.zeros((1, 4 * loads), F32)
    fetch[2].wait()
    load[...] = wide([rigid[3 * (g % 2):3 * (g % 2) + 3, g // 2, :] for g in range(4)], no_row)
    for buf in (rx, x0, x1, x2):
        blank(buf)
    for n, (_, _, come) in enumerate(near):
        @pl.when(jnp.logical_not(come))
        def _(n=n):
            kall[n] = jnp.zeros(kall.shape[1:], F32)
            tin[0, n] = jnp.zeros(tin.shape[2:], F32)
            tin[1, n] = jnp.zeros(tin.shape[2:], F32)
    wf[...] = jnp.zeros(wf.shape, F32)
    for l, f in both:
        wf[l, f, 8 * l:8 * l + 8] = rw[f, l]
    wf[0, 3, 8:16] = rw[2, 1]
    wf[1, 2, 0:8] = rw[3, 0]

    pl.semaphore_wait(barrier, n_dev - 1)

    rcopies = exchange(rw, rx, 3)
    begin(rcopies)
    own_a = gather_start(load, 0)
    fetch[3].wait()
    own = inverse.shape[0]
    half = own // 2
    group = 32 if n_dev % 32 == 0 else n_dev
    cols = lax.broadcasted_iota(jnp.int32, (own * group, 4 * group), 0)
    slot = lax.broadcasted_iota(jnp.int32, (own * group, 4 * group), 1)
    base = own * (slot // 4) + lax.rem(slot, 4)
    picks = [jnp.where((lax.rem(slot, 4) < 3) & (cols == base + 3 * g), 1.0, 0.0).astype(BF) for g in range(4)]
    for n in range(n_dev // group):
        pad = jnp.zeros((8 - half, own * group), F32)
        part = inverse[:, n * own * group:(n + 1) * own * group]
        part = jnp.concatenate([part[0:half], pad, part[half:own], pad], axis=0)
        stack = jnp.concatenate(three(part), axis=0)
        for g in range(4):
            r = dot(stack, picks[g])
            kin[g, :, n * 4 * group:(n + 1) * 4 * group] = r[0:16] + r[16:32] + r[32:48]
    kcopies = swap([kin] * 4, kall, kx_send, kx_recv)
    begin(kcopies)

    def doubled(x):
        return jnp.concatenate(two(x), axis=0)

    def folded(r):
        n = r.shape[0] // 2
        return r[0:n] + r[n:2 * n]

    def squared(r):
        r = folded(r)
        return r[:, 0:loads] + r[:, loads:2 * loads]

    index = jnp.concatenate([fmap[0], fmap[1]], axis=0).astype(F32).T.astype(jnp.int32)
    for l, f in both:
        lane = lax.broadcasted_iota(jnp.int32, (width, unk), 1)
        sign = -1.0 if f in (0, 2) else 1.0
        ptt[l, width * f:width * f + width] = jnp.where(
            lane == index[:, 4 * l + f:4 * l + f + 1], sign, 0.0).astype(BF)

    fetch[4].wait()
    for l in range(2):
        stack = doubled(free[l])
        for f in range(4):
            z0[f, l] = folded(dot(stack, pt[l, f]))

    finish(rcopies, False)
    for l in range(2):
        wf[l, 0, 16 + 8 * l:24 + 8 * l] = rx[0, l]
        wf[l, 1, 32 + 8 * l:40 + 8 * l] = rx[1, l]
    wf[0, 2, 48:56] = rx[2, 0]
    wf[1, 3, 56:64] = rx[3, 1]
    for l, f in both:
        wlift[l, f] = doubled(wf[l, f])
    s_copy.wait()
    t_free = jnp.zeros((128, 2 * loads), F32)
    cover = jnp.zeros((128, 128), F32)
    for l in range(2):
        y = dot(jnp.concatenate([wlift[l, f] for f in range(4)], axis=1), ptt[l]).astype(BF)
        ybuf[l] = y
        t_free += dot(y, doubled(free[l]), NT)
        v = doubled(folded(dot(y, s_buf[l])))
        ysb[l] = v
        cover += dot(v, y, NT)
    bst[...] = doubled(folded(cover))
    tzero[0] = squared(t_free)

    finish(kcopies, False)
    for g in range(4):
        rows = lax.broadcasted_iota(jnp.int32, (64, nr), 0)
        lane = lax.broadcasted_iota(jnp.int32, (64, nr), 1)
        k = jnp.concatenate([kin[g], kall[0, g], kall[1, g], kall[2, g, 8:16], kall[3, g, 0:8]], axis=0)
        h, o = two(jnp.where((rows == 8 * g + 6) & (lax.rem(lane, 4) == 3), 1.0, k))
        for n, v in enumerate((h, h, o, o)):
            kn[64 * n:64 * n + 64, g * nr:(g + 1) * nr] = v

    def coarse(own, phase):
        gather_finish(own, phase)
        gt = gath[phase].reshape(nr, 128).T
        x = jnp.concatenate([gt[0:32], gt[32:64], gt[64:96], gt[96:128]], axis=1)
        r = folded(dot(doubled(x), kn[...], NT))
        return r[:, 0:128] + r[:, 128:256]

    def send_modes(stack, phase):
        tbuf[...] = tzero[phase] - squared(dot(bst[...], stack, NT))
        nil = jnp.zeros((3, loads), F32)

        def block(a, b):
            parts = []
            for n in (a, b):
                for k in range(2):
                    parts.append(nil if n is None else tbuf[8 * n + 3 * k:8 * n + 3 * k + 3, :])
            return wide(parts, no_row)
        for n, (a, b) in enumerate(((4, 5), (2, 3), (7, None), (None, 6), (0, 1))):
            tout[phase, n] = block(a, b)
        copies = swap([tout.at[phase, n] for n in range(4)], tin.at[phase], tx_send.at[phase], tx_recv.at[phase])
        begin(copies)
        return copies

    def sum_modes(copies, phase, last):
        finish(copies, False)
        t = (tout[phase, 4] + tin[phase, 0]) + (tin[phase, 1] + tin[phase, 2]) + tin[phase, 3]
        pay[phase] = wide([t[0:3]], last)
        return gather_start(pay.at[phase], phase + 1)

    def rowsums(*fields):
        v = jnp.concatenate([x[:, 0:128] + x[:, 128:256] for x in fields], axis=0)
        n = v.shape[0]
        r = dot(jnp.ones((8, 128), BF), jnp.concatenate(three(v), axis=0), NT)
        r = r[:, 0:n] + r[:, n:2 * n] + r[:, 2 * n:3 * n]
        parts = [r[0:1, loads * k:loads * k + loads] for k in range(len(fields))]
        return jnp.concatenate(parts + [jnp.zeros((1, loads), F32)] * (4 - len(fields)), axis=1)

    def through(field, l):
        y = dot(jnp.concatenate([doubled(field[l, f]) for f in range(4)], axis=1), ptt[l])
        stack = doubled(folded(dot(y.astype(BF), s_buf[l])))
        for f in range(4):
            su[l, f] = folded(dot(stack, pt[l, f]))

    def jumped(z, x, l, f):
        if (l, f) == (0, 3):
            return z[3, 0] + z[2, 1]
        if (l, f) == (1, 2):
            return z[2, 1] + z[3, 0]
        return z[f, l] + x[f, l]

    stack = doubled(coarse(own_a, 0))
    modes0 = send_modes(stack, 0)
    copies0 = exchange(z0, x0, 0)
    for l in range(2):
        for f in range(4):
            sgb[l, f] = dot(ysb[l], pt[l, f]).astype(BF)
        for f in range(4):
            z0[f, l] = z0[f, l] - folded(dot(stack, sgb[l, f]))
        begin(copies0[3 * l:3 * l + 3])
    for l, f in both:
        mult[l, f] = folded(dot(stack, wlift[l, f]))
    own_b = sum_modes(modes0, 0, no_row)

    landing = [[n for n, side in enumerate(sides) if side[4] == l] for l in range(2)]
    t = jnp.zeros((128, 2 * loads), F32)
    for l, landed in enumerate(landing):
        finish([copies0[n] for n in landed], False)
        for f in range(4):
            r = jumped(z0, x0, l, f)
            res[l, f] = r
            t += dot(sgb[l, f], doubled(r), NT)
    tzero[1] = squared(t)
    through(res, 0)

    stack = doubled(coarse(own_b, 1))
    modes1 = send_modes(stack, 1)
    copies1 = exchange(z1, x1, 1)
    norm = jnp.zeros((32, width), F32)
    curve = jnp.zeros((32, width), F32)
    for l in range(2):
        if l == 1:
            through(res, 1)
        for f in range(4):
            z = su[l, f] - folded(dot(stack, sgb[l, f]))
            z1[f, l] = z
            p = res[l, f] - folded(dot(stack, wlift[l, f]))
            d0[l, f] = p
            norm += p * p
            curve += p * z
        begin(copies1[3 * l:3 * l + 3])
    own_c = sum_modes(modes1, 1, rowsums(norm, 2.0 * curve))

    for l, landed in enumerate(landing):
        finish([copies1[n] for n in landed], False)
        for f in range(4):
            w0[l, f] = jumped(z1, x1, l, f)
        through(w0, l)

    c = coarse(own_c, 2)
    stack = doubled(c)
    norm0 = c[:, 6:7]
    curve0 = c[:, 14:15]
    step0 = norm0 / curve0
    norm = jnp.zeros((32, width), F32)
    curve = jnp.zeros((32, width), F32)
    cross = jnp.zeros((32, width), F32)
    copies2 = exchange(z2, x2, 2)
    for l, f in both:
        p = d0[l, f] - step0 * (w0[l, f] - folded(dot(stack, wlift[l, f])))
        z = z1[f, l] - step0 * (su[l, f] - folded(dot(stack, sgb[l, f])))
        p1[l, f] = p
        z2[f, l] = z
        norm += p * p
        curve += p * z
        cross += p * z1[f, l]
    pay[2] = wide([jnp.zeros((3, 4 * loads), F32)], rowsums(norm, 2.0 * curve, 2.0 * cross))
    own_d = gather_start(pay.at[2], 3)
    begin(copies2)
    for l, f in both:
        mult[l, f] = mult[l, f] + step0 * d0[l, f]
        res[l, f] = res[l, f] - step0 * w0[l, f]
    finish(copies2, False)
    gather_finish(own_d, 3)
    total = jnp.sum(gath[3], axis=0)
    total = jnp.concatenate([total, jnp.zeros(total.shape, F32)], axis=0).T
    norm1, half1, cross1 = [total[loads * k:loads * k + loads, 3:4] for k in range(3)]
    beta = norm1 / norm0
    curve1 = half1 + 2.0 * beta * cross1 + beta * beta * curve0
    step1 = norm1 / curve1
    for l, f in both:
        mult_out[l, f] = mult[l, f] + step1 * (p1[l, f] + beta * d0[l, f])
        res_out[l, f] = res[l, f] - step1 * (jumped(z2, x2, l, f) + beta * w0[l, f])
    for group in (rcopies, kcopies, modes0, modes1, copies0, copies1, copies2):
        finish(group, True)
    for phase in range(4):
        many = gath.at[phase, pl.ds(0, n_dev - 1)]
        pltpu.make_async_copy(many, many, ag_send.at[phase]).wait()


def hand_over(mult, res, mult_out, res_out, sem):
    copies = [pltpu.make_async_copy(a, b, sem.at[n]) for n, (a, b) in enumerate(((mult, mult_out), (res, res_out)))]
    for c in copies:
        c.start()
    for c in copies:
        c.wait()


def local(n_sub, n_grp, schur, free, traces, load, coarse_inverse, face_map):
    n_dev = n_sub * n_grp
    loads, unk = free.shape[1], free.shape[2]
    width = face_map.shape[2]
    nr = 4 * n_dev
    vm = pl.BlockSpec(memory_space=pltpu.VMEM)
    hbm = pl.BlockSpec(memory_space=pl.ANY)
    field = pltpu.VMEM((2, 4, loads, width), F32)
    face = pltpu.VMEM((4, 2, loads, width), F32)
    dma = pltpu.SemaphoreType.DMA
    out = jax.ShapeDtypeStruct((2, 4, loads, width), F32)
    held = pltpu.VMEM((2, 4, loads, width), F32)
    results = pl.pallas_call(
        functools.partial(kernel, n_sub, n_grp),
        out_shape=(held, held),
        in_specs=[hbm] * 6,
        out_specs=(vm, vm),
        scratch_shapes=[
            pltpu.VMEM(free.shape, F32),
            pltpu.VMEM((traces.shape[1], 2, unk), F32),
            pltpu.VMEM((load.shape[1], 2, loads), F32),
            pltpu.VMEM(coarse_inverse.shape, F32),
            pltpu.VMEM(face_map.shape, jnp.int32),
            pltpu.VMEM((2, unk, unk), BF),
            pltpu.VMEM((2, 4, unk, width), BF),
            pltpu.VMEM((2, 4 * width, unk), BF),
            pltpu.VMEM((2, 128, unk), BF),
            pltpu.VMEM((2, 128, unk), BF),
            pltpu.VMEM((2, 4, 128, width), BF),
            pltpu.VMEM((4, 2, 8, width), F32),
            pltpu.VMEM((4, 2, 8, width), F32),
            pltpu.VMEM((4, 16, nr), F32),
            pltpu.VMEM((4, 4, 16, nr), F32),
            pltpu.VMEM((256, 4 * nr), BF),
            pltpu.VMEM((2, 4, 64, width), F32),
            pltpu.VMEM((2, 4, 128, width), BF),
            pltpu.VMEM((128, 128), BF),
            pltpu.VMEM((64, loads), F32),
            pltpu.VMEM((2, 64, loads), F32),
            pltpu.VMEM((2, 5, 4, 4 * loads), F32),
            pltpu.VMEM((2, 4, 4, 4 * loads), F32),
            field, field, field, field, field, field,
            face, face, face, face, face, face,
            pltpu.VMEM((4, 4 * loads), F32),
            pltpu.VMEM((3, 4, 4 * loads), F32),
            pltpu.VMEM((4, n_dev, 4, 4 * loads), F32),
            dma, dma((5,)), dma((4,)), dma((4,)), dma((4,)), dma((4, 6)), dma((4, 6)), dma((4,)), dma((4,)),
            dma((2, 4)), dma((2, 4)),
        ],
        compiler_params=pltpu.CompilerParams(
            collective_id=0, has_side_effects=True, vmem_limit_bytes=56 * 1024 * 1024),
    )(schur, free, traces.transpose(1, 0, 2), load.transpose(1, 0, 2), coarse_inverse, face_map)
    return pl.pallas_call(
        hand_over, out_shape=(out, out), in_specs=[vm] * 2, out_specs=(hbm, hbm),
        scratch_shapes=[dma((2,))],
        compiler_params=pltpu.CompilerParams(vmem_limit_bytes=8 * 1024 * 1024))(*results)


def solution(mesh):
    both = ("sub", "grp")
    three_d = P(both, None, None)
    out = P(both, None, None, None)
    return jax.shard_map(
        functools.partial(local, mesh.shape["sub"], mesh.shape["grp"]), mesh=mesh,
        in_specs=(three_d, three_d, three_d, three_d, P(both, None), three_d),
        out_specs=(out, out), check_vma=False)
```

```python
import functools

import jax
import jax.numpy as jnp
from jax import lax
from jax.experimental import pallas as pl
from jax.experimental.pallas import tpu as pltpu
from jax.sharding import PartitionSpec as P

BF = jnp.bfloat16
F32 = jnp.float32
MESH = pl.DeviceIdType.MESH
NT = (((1,), (1,)), ((), ()))
NN = (((1,), (0,)), ((), ()))


def two(x):
    hi = x.astype(BF)
    return hi, (x - hi.astype(F32)).astype(BF)


def three(x):
    hi = x.astype(BF)
    rest = x - hi.astype(F32)
    mid = rest.astype(BF)
    return hi, mid, (rest - mid.astype(F32)).astype(BF)


def dot(a, b, dims=NN):
    return lax.dot_general(a, b, dims, preferred_element_type=F32)


def kernel(n_sub, n_grp, schur, free_in, traces_in, rigid_in, inverse_in, fmap_in, mult_out, res_out,
           free, traces, rigid, inverse, fmap, s_buf, pt, ptt, ybuf, ysb, sgb, rows, rw, rx, kin, kall, kn, wf, wlift, bst, tbuf, tzero, tout, tin,
           mult, res, d0, w0, p1, su, z0, z1, z2, x0, x1, x2, load, pay, gath,
           s_sem, in_sem, ag_send, ag_recv, ag_loc, ex_send, ex_recv, kx_send, kx_recv, tx_send, tx_recv):
    n_dev = n_sub * n_grp
    i_sub = lax.axis_index("sub")
    i_grp = lax.axis_index("grp")
    me = i_sub * n_grp + i_grp
    loads = free.shape[1]
    unk = free.shape[2]
    width = fmap.shape[2]
    nr = 4 * n_dev
    both = [(l, f) for l in range(2) for f in range(4)]

    pairs = ((fmap_in, fmap), (traces_in, traces), (rigid_in, rigid), (inverse_in, inverse), (free_in, free))
    fetch = [pltpu.make_async_copy(a, b, in_sem.at[n]) for n, (a, b) in enumerate(pairs)]
    for copy in fetch:
        copy.start()
    s_copy = pltpu.make_async_copy(schur, s_buf, s_sem)
    s_copy.start()

    barrier = pltpu.get_barrier_semaphore()

    def greet(r, carry):
        other = lax.rem(me + r, n_dev)
        pl.semaphore_signal(barrier, inc=1, device_id=(other // n_grp, lax.rem(other, n_grp)),
                            device_id_type=MESH)
        return carry
    lax.fori_loop(1, n_dev, greet, 0)

    fetch[0].wait()
    for l, f in both:
        row = fmap[l, f:f + 1, :]
        place = lax.broadcasted_iota(jnp.int32, (unk, width), 0)
        sign = -1.0 if f in (0, 2) else 1.0
        pt[l, f] = jnp.where(place == row, sign, 0.0).astype(BF)

    fetch[1].wait()
    for l in range(2):
        h, m, o = three(traces[:, l, :])
        pad = jnp.zeros((2, unk), BF)
        stack = jnp.concatenate([h, pad, m, pad, o, pad], axis=0)
        for f in range(4):
            r = dot(stack, pt[l, f])
            rw[f, l] = r[0:8] + r[8:16] + r[16:24]

    low_sub = i_sub > 0
    up_sub = i_sub < n_sub - 1
    low_grp = i_grp > 0
    up_grp = i_grp < n_grp - 1
    near = (
        (up_sub, (i_sub + 1, i_grp), low_sub),
        (low_sub, (i_sub - 1, i_grp), up_sub),
        (up_grp, (i_sub, i_grp + 1), low_grp),
        (low_grp, (i_sub, i_grp - 1), up_grp),
    )
    sides = (
        (near[0], 1, 0, 0, 0),
        (near[1], 0, 0, 1, 0),
        (near[3], 2, 0, 3, 1),
        (near[0], 1, 1, 0, 1),
        (near[1], 0, 1, 1, 1),
        (near[2], 3, 1, 2, 0),
    )

    def blank(buf):
        for (_, _, come), _, _, land, l_land in sides:
            @pl.when(jnp.logical_not(come))
            def _():
                buf[land, l_land] = jnp.zeros(buf.shape[2:], F32)

    def exchange(src, buf, phase):
        copies = []
        for n, ((there, device, come), face, l_src, land, l_land) in enumerate(sides):
            copies.append((pltpu.make_async_remote_copy(
                src_ref=src.at[face, l_src], dst_ref=buf.at[land, l_land],
                send_sem=ex_send.at[phase, n], recv_sem=ex_recv.at[phase, n],
                device_id=device, device_id_type=MESH), there, come))
        return copies

    def swap(sources, buf, send_sem, recv_sem):
        return [(pltpu.make_async_remote_copy(
            src_ref=sources[n], dst_ref=buf.at[n], send_sem=send_sem.at[n], recv_sem=recv_sem.at[n],
            device_id=device, device_id_type=MESH), there, come)
            for n, (there, device, come) in enumerate(near)]

    def begin(copies):
        for c, there, _ in copies:
            @pl.when(there)
            def _(c=c):
                c.start()

    def finish(copies, send):
        for c, there, come in copies:
            if send:
                @pl.when(there)
                def _(c=c):
                    c.wait_send()
            else:
                @pl.when(come)
                def _(c=c):
                    c.wait_recv()

    turn = 1 - 2 * (i_sub // (n_sub // 2))

    def gather_start(src, phase):
        own = pltpu.make_async_copy(src, gath.at[phase, me], ag_loc.at[phase])
        own.start()

        def send(n, carry):
            row = lax.rem(i_sub + turn * (n_sub - 1 - n) + n_sub, n_sub)
            for k in range(n_grp - 1, -1, -1):
                def one():
                    pltpu.make_async_remote_copy(
                        src_ref=src, dst_ref=gath.at[phase, me], send_sem=ag_send.at[phase],
                        recv_sem=ag_recv.at[phase], device_id=(row, lax.rem(i_grp + k, n_grp)),
                        device_id_type=MESH).start()
                if k == 0:
                    pl.when(n < n_sub - 1)(one)
                else:
                    one()
            return carry
        lax.fori_loop(0, n_sub, send, 0)
        return own

    def gather_finish(own, phase):
        own.wait()
        many = gath.at[phase, pl.ds(0, n_dev - 1)]
        pltpu.make_async_copy(many, many, ag_recv.at[phase]).wait()

    def wide(parts, last):
        return jnp.concatenate([jnp.concatenate(parts, axis=1), last], axis=0)

    no_row = jnp.zeros((1, 4 * loads), F32)
    fetch[2].wait()
    load[...] = wide([rigid[3 * (g % 2):3 * (g % 2) + 3, g // 2, :] for g in range(4)], no_row)
    for buf in (rx, x0, x1, x2):
        blank(buf)
    for n, (_, _, come) in enumerate(near):
        @pl.when(jnp.logical_not(come))
        def _(n=n):
            kall[n] = jnp.zeros(kall.shape[1:], F32)
            tin[0, n] = jnp.zeros(tin.shape[2:], F32)
            tin[1, n] = jnp.zeros(tin.shape[2:], F32)
    wf[...] = jnp.zeros(wf.shape, F32)
    for l, f in both:
        wf[l, f, 8 * l:8 * l + 8] = rw[f, l]
    wf[0, 3, 8:16] = rw[2, 1]
    wf[1, 2, 0:8] = rw[3, 0]

    pl.semaphore_wait(barrier, n_dev - 1)

    rcopies = exchange(rw, rx, 3)
    begin(rcopies)
    own_a = gather_start(load, 0)
    fetch[3].wait()
    own = inverse.shape[0]
    half = own // 2
    group = 32 if n_dev % 32 == 0 else n_dev
    cols = lax.broadcasted_iota(jnp.int32, (own * group, 4 * group), 0)
    slot = lax.broadcasted_iota(jnp.int32, (own * group, 4 * group), 1)
    base = own * (slot // 4) + lax.rem(slot, 4)
    picks = [jnp.where((lax.rem(slot, 4) < 3) & (cols == base + 3 * g), 1.0, 0.0).astype(BF) for g in range(4)]
    for n in range(n_dev // group):
        pad = jnp.zeros((8 - half, own * group), F32)
        part = inverse[:, n * own * group:(n + 1) * own * group]
        part = jnp.concatenate([part[0:half], pad, part[half:own], pad], axis=0)
        stack = jnp.concatenate(three(part), axis=0)
        for g in range(4):
            r = dot(stack, picks[g])
            kin[g, :, n * 4 * group:(n + 1) * 4 * group] = r[0:16] + r[16:32] + r[32:48]
    kcopies = swap([kin] * 4, kall, kx_send, kx_recv)
    begin(kcopies)

    def doubled(x):
        return jnp.concatenate(two(x), axis=0)

    def folded(r):
        n = r.shape[0] // 2
        return r[0:n] + r[n:2 * n]

    def squared(r):
        r = folded(r)
        return r[:, 0:loads] + r[:, loads:2 * loads]

    index = jnp.concatenate([fmap[0], fmap[1]], axis=0).astype(F32).T.astype(jnp.int32)
    for l, f in both:
        lane = lax.broadcasted_iota(jnp.int32, (width, unk), 1)
        sign = -1.0 if f in (0, 2) else 1.0
        ptt[l, width * f:width * f + width] = jnp.where(
            lane == index[:, 4 * l + f:4 * l + f + 1], sign, 0.0).astype(BF)

    fetch[4].wait()
    for l in range(2):
        stack = doubled(free[l])
        for f in range(4):
            z0[f, l] = folded(dot(stack, pt[l, f]))

    finish(rcopies, False)
    for l in range(2):
        wf[l, 0, 16 + 8 * l:24 + 8 * l] = rx[0, l]
        wf[l, 1, 32 + 8 * l:40 + 8 * l] = rx[1, l]
    wf[0, 2, 48:56] = rx[2, 0]
    wf[1, 3, 56:64] = rx[3, 1]
    for l, f in both:
        wlift[l, f] = doubled(wf[l, f])
    s_copy.wait()
    t_free = jnp.zeros((128, 2 * loads), F32)
    cover = jnp.zeros((128, 128), F32)
    for l in range(2):
        y = dot(jnp.concatenate([wlift[l, f] for f in range(4)], axis=1), ptt[l]).astype(BF)
        ybuf[l] = y
        t_free += dot(y, doubled(free[l]), NT)
        v = doubled(folded(dot(y, s_buf[l])))
        ysb[l] = v
        cover += dot(v, y, NT)
    bst[...] = doubled(folded(cover))
    tzero[0] = squared(t_free)

    finish(kcopies, False)
    for g in range(4):
        place = lax.broadcasted_iota(jnp.int32, (64, nr), 0)
        lane = lax.broadcasted_iota(jnp.int32, (64, nr), 1)
        k = jnp.concatenate([kin[g], kall[0, g], kall[1, g], kall[2, g, 8:16], kall[3, g, 0:8]], axis=0)
        h, o = two(jnp.where((place == 8 * g + 6) & (lax.rem(lane, 4) == 3), 1.0, k))
        for n, v in enumerate((h, h, o, o)):
            kn[64 * n:64 * n + 64, g * nr:(g + 1) * nr] = v

    def coarse(own, phase):
        gather_finish(own, phase)
        gt = gath[phase].reshape(nr, 128).T
        x = jnp.concatenate([gt[0:32], gt[32:64], gt[64:96], gt[96:128]], axis=1)
        r = folded(dot(doubled(x), kn[...], NT))
        return r[:, 0:128] + r[:, 128:256]

    def send_modes(stack, phase):
        tbuf[...] = tzero[phase] - squared(dot(bst[...], stack, NT))
        nil = jnp.zeros((3, loads), F32)

        def block(a, b):
            parts = []
            for n in (a, b):
                for k in range(2):
                    parts.append(nil if n is None else tbuf[8 * n + 3 * k:8 * n + 3 * k + 3, :])
            return wide(parts, no_row)
        for n, (a, b) in enumerate(((4, 5), (2, 3), (7, None), (None, 6), (0, 1))):
            tout[phase, n] = block(a, b)
        copies = swap([tout.at[phase, n] for n in range(4)], tin.at[phase], tx_send.at[phase], tx_recv.at[phase])
        begin(copies)
        return copies

    def sum_modes(copies, phase, last):
        finish(copies, False)
        t = (tout[phase, 4] + tin[phase, 0]) + (tin[phase, 1] + tin[phase, 2]) + tin[phase, 3]
        pay[phase] = wide([t[0:3]], last)
        return gather_start(pay.at[phase], phase + 1)

    def rowsums(*fields):
        v = jnp.concatenate([x[:, 0:128] + x[:, 128:256] for x in fields], axis=0)
        n = v.shape[0]
        r = dot(jnp.ones((8, 128), BF), jnp.concatenate(three(v), axis=0), NT)
        r = r[:, 0:n] + r[:, n:2 * n] + r[:, 2 * n:3 * n]
        parts = [r[0:1, loads * k:loads * k + loads] for k in range(len(fields))]
        return jnp.concatenate(parts + [jnp.zeros((1, loads), F32)] * (4 - len(fields)), axis=1)

    def through(rows, l):
        y = dot(rows, ptt[l])
        stack = doubled(folded(dot(y.astype(BF), s_buf[l])))
        for f in range(4):
            su[l, f] = folded(dot(stack, pt[l, f]))

    def jumped(z, x, l, f):
        if (l, f) == (0, 3):
            return z[3, 0] + z[2, 1]
        if (l, f) == (1, 2):
            return z[2, 1] + z[3, 0]
        return z[f, l] + x[f, l]

    stack = doubled(coarse(own_a, 0))
    modes0 = send_modes(stack, 0)
    copies0 = exchange(z0, x0, 0)
    for l in range(2):
        for f in range(4):
            sgb[l, :, width * f:width * f + width] = dot(ysb[l], pt[l, f]).astype(BF)
        for f in range(4):
            z0[f, l] = z0[f, l] - folded(dot(stack, sgb[l, :, width * f:width * f + width]))
        begin(copies0[3 * l:3 * l + 3])
    for l, f in both:
        mult[l, f] = folded(dot(stack, wlift[l, f]))
    own_b = sum_modes(modes0, 0, no_row)

    landing = [[n for n, side in enumerate(sides) if side[4] == l] for l in range(2)]
    t = jnp.zeros((128, 2 * loads), F32)
    for l, landed in enumerate(landing):
        finish([copies0[n] for n in landed], False)
        for f in range(4):
            r = jumped(z0, x0, l, f)
            res[l, f] = r
            rows[l, :, width * f:width * f + width] = doubled(r)
        t += dot(sgb[l], rows[l], NT)
    tzero[1] = squared(t)
    through(rows[0], 0)

    stack = doubled(coarse(own_b, 1))
    modes1 = send_modes(stack, 1)
    copies1 = exchange(z1, x1, 1)
    norm = jnp.zeros((32, width), F32)
    curve = jnp.zeros((32, width), F32)
    for l in range(2):
        if l == 1:
            through(rows[1], 1)
        for f in range(4):
            z = su[l, f] - folded(dot(stack, sgb[l, :, width * f:width * f + width]))
            z1[f, l] = z
            p = res[l, f] - folded(dot(stack, wlift[l, f]))
            d0[l, f] = p
            norm += p * p
            curve += p * z
        begin(copies1[3 * l:3 * l + 3])
    own_c = sum_modes(modes1, 1, rowsums(norm, 2.0 * curve))

    for l, landed in enumerate(landing):
        finish([copies1[n] for n in landed], False)
        for f in range(4):
            w = jumped(z1, x1, l, f)
            w0[l, f] = w
            rows[l, :, width * f:width * f + width] = doubled(w)
        through(rows[l], l)

    c = coarse(own_c, 2)
    stack = doubled(c)
    norm0 = c[:, 6:7]
    curve0 = c[:, 14:15]
    step0 = norm0 / curve0
    norm = jnp.zeros((32, width), F32)
    curve = jnp.zeros((32, width), F32)
    cross = jnp.zeros((32, width), F32)
    copies2 = exchange(z2, x2, 2)
    for l, f in both:
        p = d0[l, f] - step0 * (w0[l, f] - folded(dot(stack, wlift[l, f])))
        z = z1[f, l] - step0 * (su[l, f] - folded(dot(stack, sgb[l, :, width * f:width * f + width])))
        p1[l, f] = p
        z2[f, l] = z
        norm += p * p
        curve += p * z
        cross += p * z1[f, l]
    pay[2] = wide([jnp.zeros((3, 4 * loads), F32)], rowsums(norm, 2.0 * curve, 2.0 * cross))
    own_d = gather_start(pay.at[2], 3)
    begin(copies2)
    for l, f in both:
        mult[l, f] = mult[l, f] + step0 * d0[l, f]
        res[l, f] = res[l, f] - step0 * w0[l, f]
    finish(copies2, False)
    gather_finish(own_d, 3)
    total = jnp.sum(gath[3], axis=0)
    total = jnp.concatenate([total, jnp.zeros(total.shape, F32)], axis=0).T
    norm1, half1, cross1 = [total[loads * k:loads * k + loads, 3:4] for k in range(3)]
    beta = norm1 / norm0
    curve1 = half1 + 2.0 * beta * cross1 + beta * beta * curve0
    step1 = norm1 / curve1
    for l, f in both:
        mult_out[l, f] = mult[l, f] + step1 * (p1[l, f] + beta * d0[l, f])
        res_out[l, f] = res[l, f] - step1 * (jumped(z2, x2, l, f) + beta * w0[l, f])
    for group in (rcopies, kcopies, modes0, modes1, copies0, copies1, copies2):
        finish(group, True)
    for phase in range(4):
        many = gath.at[phase, pl.ds(0, n_dev - 1)]
        pltpu.make_async_copy(many, many, ag_send.at[phase]).wait()


def hand_over(mult, res, mult_out, res_out, sem):
    copies = [pltpu.make_async_copy(a, b, sem.at[n]) for n, (a, b) in enumerate(((mult, mult_out), (res, res_out)))]
    for c in copies:
        c.start()
    for c in copies:
        c.wait()


def local(n_sub, n_grp, schur, free, traces, load, coarse_inverse, face_map):
    n_dev = n_sub * n_grp
    loads, unk = free.shape[1], free.shape[2]
    width = face_map.shape[2]
    nr = 4 * n_dev
    vm = pl.BlockSpec(memory_space=pltpu.VMEM)
    hbm = pl.BlockSpec(memory_space=pl.ANY)
    field = pltpu.VMEM((2, 4, loads, width), F32)
    face = pltpu.VMEM((4, 2, loads, width), F32)
    dma = pltpu.SemaphoreType.DMA
    out = jax.ShapeDtypeStruct((2, 4, loads, width), F32)
    held = pltpu.VMEM((2, 4, loads, width), F32)
    results = pl.pallas_call(
        functools.partial(kernel, n_sub, n_grp),
        out_shape=(held, held),
        in_specs=[hbm] * 6,
        out_specs=(vm, vm),
        scratch_shapes=[
            pltpu.VMEM(free.shape, F32),
            pltpu.VMEM((traces.shape[1], 2, unk), F32),
            pltpu.VMEM((load.shape[1], 2, loads), F32),
            pltpu.VMEM(coarse_inverse.shape, F32),
            pltpu.VMEM(face_map.shape, jnp.int32),
            pltpu.VMEM((2, unk, unk), BF),
            pltpu.VMEM((2, 4, unk, width), BF),
            pltpu.VMEM((2, 4 * width, unk), BF),
            pltpu.VMEM((2, 128, unk), BF),
            pltpu.VMEM((2, 128, unk), BF),
            pltpu.VMEM((2, 128, 4 * width), BF),
            pltpu.VMEM((2, 2 * loads, 4 * width), BF),
            pltpu.VMEM((4, 2, 8, width), F32),
            pltpu.VMEM((4, 2, 8, width), F32),
            pltpu.VMEM((4, 16, nr), F32),
            pltpu.VMEM((4, 4, 16, nr), F32),
            pltpu.VMEM((256, 4 * nr), BF),
            pltpu.VMEM((2, 4, 64, width), F32),
            pltpu.VMEM((2, 4, 128, width), BF),
            pltpu.VMEM((128, 128), BF),
            pltpu.VMEM((64, loads), F32),
            pltpu.VMEM((2, 64, loads), F32),
            pltpu.VMEM((2, 5, 4, 4 * loads), F32),
            pltpu.VMEM((2, 4, 4, 4 * loads), F32),
            field, field, field, field, field, field,
            face, face, face, face, face, face,
            pltpu.VMEM((4, 4 * loads), F32),
            pltpu.VMEM((3, 4, 4 * loads), F32),
            pltpu.VMEM((4, n_dev, 4, 4 * loads), F32),
            dma, dma((5,)), dma((4,)), dma((4,)), dma((4,)), dma((4, 6)), dma((4, 6)), dma((4,)), dma((4,)),
            dma((2, 4)), dma((2, 4)),
        ],
        compiler_params=pltpu.CompilerParams(
            collective_id=0, has_side_effects=True, vmem_limit_bytes=56 * 1024 * 1024),
    )(schur, free, traces.transpose(1, 0, 2), load.transpose(1, 0, 2), coarse_inverse, face_map)
    return pl.pallas_call(
        hand_over, out_shape=(out, out), in_specs=[vm] * 2, out_specs=(hbm, hbm),
        scratch_shapes=[dma((2,))],
        compiler_params=pltpu.CompilerParams(vmem_limit_bytes=8 * 1024 * 1024))(*results)


def solution(mesh):
    both = ("sub", "grp")
    three_d = P(both, None, None)
    out = P(both, None, None, None)
    return jax.shard_map(
        functools.partial(local, mesh.shape["sub"], mesh.shape["grp"]), mesh=mesh,
        in_specs=(three_d, three_d, three_d, three_d, P(both, None), three_d),
        out_specs=(out, out), check_vma=False)
```

```python
import functools

import jax
import jax.numpy as jnp
from jax import lax
from jax.experimental import pallas as pl
from jax.experimental.pallas import tpu as pltpu
from jax.sharding import PartitionSpec as P

BF = jnp.bfloat16
F32 = jnp.float32
MESH = pl.DeviceIdType.MESH
NT = (((1,), (1,)), ((), ()))
NN = (((1,), (0,)), ((), ()))


def two(x):
    hi = x.astype(BF)
    return hi, (x - hi.astype(F32)).astype(BF)


def three(x):
    hi = x.astype(BF)
    rest = x - hi.astype(F32)
    mid = rest.astype(BF)
    return hi, mid, (rest - mid.astype(F32)).astype(BF)


def dot(a, b, dims=NN):
    return lax.dot_general(a, b, dims, preferred_element_type=F32)


def kernel(n_sub, n_grp, schur, free_in, traces_in, rigid_in, inverse_in, fmap_in, mult_out, res_out,
           free, traces, rigid, inverse, fmap, s_buf, pt, ptt, ybuf, ysb, sgb, rows, rw, rx, kin, kall, kn, wf, wlift, bst, tbuf, tzero, tout, tin,
           mult, res, d0, w0, p1, su, z0, z1, z2, x0, x1, x2, load, pay, gath,
           s_sem, in_sem, ag_send, ag_recv, ag_loc, ex_send, ex_recv, kx_send, kx_recv, tx_send, tx_recv):
    n_dev = n_sub * n_grp
    i_sub = lax.axis_index("sub")
    i_grp = lax.axis_index("grp")
    me = i_sub * n_grp + i_grp
    loads = free.shape[1]
    unk = free.shape[2]
    width = fmap.shape[2]
    nr = 4 * n_dev
    both = [(l, f) for l in range(2) for f in range(4)]

    pairs = ((fmap_in, fmap), (traces_in, traces), (rigid_in, rigid), (inverse_in, inverse), (free_in, free))
    fetch = [pltpu.make_async_copy(a, b, in_sem.at[n]) for n, (a, b) in enumerate(pairs)]
    for copy in fetch:
        copy.start()
    s_copy = pltpu.make_async_copy(schur, s_buf, s_sem)
    s_copy.start()

    barrier = pltpu.get_barrier_semaphore()

    def greet(r, carry):
        other = lax.rem(me + r, n_dev)
        pl.semaphore_signal(barrier, inc=1, device_id=(other // n_grp, lax.rem(other, n_grp)),
                            device_id_type=MESH)
        return carry
    lax.fori_loop(1, n_dev, greet, 0)

    fetch[0].wait()
    for l, f in both:
        row = fmap[l, f:f + 1, :]
        place = lax.broadcasted_iota(jnp.int32, (unk, width), 0)
        sign = -1.0 if f in (0, 2) else 1.0
        pt[l, f] = jnp.where(place == row, sign, 0.0).astype(BF)

    fetch[1].wait()
    for l in range(2):
        h, m, o = three(traces[:, l, :])
        pad = jnp.zeros((2, unk), BF)
        stack = jnp.concatenate([h, pad, m, pad, o, pad], axis=0)
        for f in range(4):
            r = dot(stack, pt[l, f])
            rw[f, l] = r[0:8] + r[8:16] + r[16:24]

    low_sub = i_sub > 0
    up_sub = i_sub < n_sub - 1
    low_grp = i_grp > 0
    up_grp = i_grp < n_grp - 1
    near = (
        (up_sub, (i_sub + 1, i_grp), low_sub),
        (low_sub, (i_sub - 1, i_grp), up_sub),
        (up_grp, (i_sub, i_grp + 1), low_grp),
        (low_grp, (i_sub, i_grp - 1), up_grp),
    )
    sides = (
        (near[0], 1, 0, 0, 0),
        (near[1], 0, 0, 1, 0),
        (near[3], 2, 0, 3, 1),
        (near[0], 1, 1, 0, 1),
        (near[1], 0, 1, 1, 1),
        (near[2], 3, 1, 2, 0),
    )

    def blank(buf):
        for (_, _, come), _, _, land, l_land in sides:
            @pl.when(jnp.logical_not(come))
            def _():
                buf[land, l_land] = jnp.zeros(buf.shape[2:], F32)

    def exchange(src, buf, phase):
        copies = []
        for n, ((there, device, come), face, l_src, land, l_land) in enumerate(sides):
            copies.append((pltpu.make_async_remote_copy(
                src_ref=src.at[face, l_src], dst_ref=buf.at[land, l_land],
                send_sem=ex_send.at[phase, n], recv_sem=ex_recv.at[phase, n],
                device_id=device, device_id_type=MESH), there, come))
        return copies

    def swap(sources, buf, send_sem, recv_sem):
        return [(pltpu.make_async_remote_copy(
            src_ref=sources[n], dst_ref=buf.at[n], send_sem=send_sem.at[n], recv_sem=recv_sem.at[n],
            device_id=device, device_id_type=MESH), there, come)
            for n, (there, device, come) in enumerate(near)]

    def begin(copies):
        for c, there, _ in copies:
            @pl.when(there)
            def _(c=c):
                c.start()

    def finish(copies, send):
        for c, there, come in copies:
            if send:
                @pl.when(there)
                def _(c=c):
                    c.wait_send()
            else:
                @pl.when(come)
                def _(c=c):
                    c.wait_recv()

    turn = 1 - 2 * (i_sub // (n_sub // 2))

    def gather_start(src, phase):
        own = pltpu.make_async_copy(src, gath.at[phase, me], ag_loc.at[phase])
        own.start()

        def send(n, carry):
            row = lax.rem(i_sub + turn * (n_sub - 1 - n) + n_sub, n_sub)
            for k in range(n_grp - 1, -1, -1):
                def one():
                    pltpu.make_async_remote_copy(
                        src_ref=src, dst_ref=gath.at[phase, me], send_sem=ag_send.at[phase],
                        recv_sem=ag_recv.at[phase], device_id=(row, lax.rem(i_grp + k, n_grp)),
                        device_id_type=MESH).start()
                if k == 0:
                    pl.when(n < n_sub - 1)(one)
                else:
                    one()
            return carry
        lax.fori_loop(0, n_sub, send, 0)
        return own

    def gather_finish(own, phase):
        own.wait()
        many = gath.at[phase, pl.ds(0, n_dev - 1)]
        pltpu.make_async_copy(many, many, ag_recv.at[phase]).wait()

    def wide(parts, last):
        return jnp.concatenate([jnp.concatenate(parts, axis=1), last], axis=0)

    no_row = jnp.zeros((1, 4 * loads), F32)
    fetch[2].wait()
    load[...] = wide([rigid[3 * (g % 2):3 * (g % 2) + 3, g // 2, :] for g in range(4)], no_row)
    pl.semaphore_wait(barrier, n_dev - 1)

    rcopies = exchange(rw, rx, 3)
    begin(rcopies)
    own_a = gather_start(load, 0)
    fetch[3].wait()
    own = inverse.shape[0]
    half = own // 2
    group = 32 if n_dev % 32 == 0 else n_dev
    cols = lax.broadcasted_iota(jnp.int32, (own * group, 4 * group), 0)
    slot = lax.broadcasted_iota(jnp.int32, (own * group, 4 * group), 1)
    base = own * (slot // 4) + lax.rem(slot, 4)
    picks = [jnp.where((lax.rem(slot, 4) < 3) & (cols == base + 3 * g), 1.0, 0.0).astype(BF) for g in range(4)]
    for n in range(n_dev // group):
        pad = jnp.zeros((8 - half, own * group), F32)
        part = inverse[:, n * own * group:(n + 1) * own * group]
        part = jnp.concatenate([part[0:half], pad, part[half:own], pad], axis=0)
        stack = jnp.concatenate(three(part), axis=0)
        for g in range(4):
            r = dot(stack, picks[g])
            kin[g, :, n * 4 * group:(n + 1) * 4 * group] = r[0:16] + r[16:32] + r[32:48]
    kcopies = swap([kin] * 4, kall, kx_send, kx_recv)
    begin(kcopies)
    for buf in (rx, x0, x1, x2):
        blank(buf)
    for n, (_, _, come) in enumerate(near):
        @pl.when(jnp.logical_not(come))
        def _(n=n):
            kall[n] = jnp.zeros(kall.shape[1:], F32)
            tin[0, n] = jnp.zeros(tin.shape[2:], F32)
            tin[1, n] = jnp.zeros(tin.shape[2:], F32)
    wf[...] = jnp.zeros(wf.shape, F32)
    for l, f in both:
        wf[l, f, 8 * l:8 * l + 8] = rw[f, l]
    wf[0, 3, 8:16] = rw[2, 1]
    wf[1, 2, 0:8] = rw[3, 0]


    def doubled(x):
        return jnp.concatenate(two(x), axis=0)

    def folded(r):
        n = r.shape[0] // 2
        return r[0:n] + r[n:2 * n]

    def squared(r):
        r = folded(r)
        return r[:, 0:loads] + r[:, loads:2 * loads]

    index = jnp.concatenate([fmap[0], fmap[1]], axis=0).astype(F32).T.astype(jnp.int32)
    for l, f in both:
        lane = lax.broadcasted_iota(jnp.int32, (width, unk), 1)
        sign = -1.0 if f in (0, 2) else 1.0
        ptt[l, width * f:width * f + width] = jnp.where(
            lane == index[:, 4 * l + f:4 * l + f + 1], sign, 0.0).astype(BF)

    fetch[4].wait()
    for l in range(2):
        stack = doubled(free[l])
        for f in range(4):
            z0[f, l] = folded(dot(stack, pt[l, f]))

    finish(rcopies, False)
    for l in range(2):
        wf[l, 0, 16 + 8 * l:24 + 8 * l] = rx[0, l]
        wf[l, 1, 32 + 8 * l:40 + 8 * l] = rx[1, l]
    wf[0, 2, 48:56] = rx[2, 0]
    wf[1, 3, 56:64] = rx[3, 1]
    for l, f in both:
        wlift[l, f] = doubled(wf[l, f])
    s_copy.wait()
    t_free = jnp.zeros((128, 2 * loads), F32)
    cover = jnp.zeros((128, 128), F32)
    for l in range(2):
        y = dot(jnp.concatenate([wlift[l, f] for f in range(4)], axis=1), ptt[l]).astype(BF)
        ybuf[l] = y
        t_free += dot(y, doubled(free[l]), NT)
        v = doubled(folded(dot(y, s_buf[l])))
        ysb[l] = v
        cover += dot(v, y, NT)
    bst[...] = doubled(folded(cover))
    tzero[0] = squared(t_free)

    finish(kcopies, False)
    for g in range(4):
        place = lax.broadcasted_iota(jnp.int32, (64, nr), 0)
        lane = lax.broadcasted_iota(jnp.int32, (64, nr), 1)
        k = jnp.concatenate([kin[g], kall[0, g], kall[1, g], kall[2, g, 8:16], kall[3, g, 0:8]], axis=0)
        h, o = two(jnp.where((place == 8 * g + 6) & (lax.rem(lane, 4) == 3), 1.0, k))
        for n, v in enumerate((h, h, o, o)):
            kn[64 * n:64 * n + 64, g * nr:(g + 1) * nr] = v

    def coarse(own, phase):
        gather_finish(own, phase)
        gt = gath[phase].reshape(nr, 128).T
        x = jnp.concatenate([gt[0:32], gt[32:64], gt[64:96], gt[96:128]], axis=1)
        r = folded(dot(doubled(x), kn[...], NT))
        return r[:, 0:128] + r[:, 128:256]

    def send_modes(stack, phase):
        tbuf[...] = tzero[phase] - squared(dot(bst[...], stack, NT))
        nil = jnp.zeros((3, loads), F32)

        def block(a, b):
            parts = []
            for n in (a, b):
                for k in range(2):
                    parts.append(nil if n is None else tbuf[8 * n + 3 * k:8 * n + 3 * k + 3, :])
            return wide(parts, no_row)
        for n, (a, b) in enumerate(((4, 5), (2, 3), (7, None), (None, 6), (0, 1))):
            tout[phase, n] = block(a, b)
        copies = swap([tout.at[phase, n] for n in range(4)], tin.at[phase], tx_send.at[phase], tx_recv.at[phase])
        begin(copies)
        return copies

    def sum_modes(copies, phase, last):
        finish(copies, False)
        t = (tout[phase, 4] + tin[phase, 0]) + (tin[phase, 1] + tin[phase, 2]) + tin[phase, 3]
        pay[phase] = wide([t[0:3]], last)
        return gather_start(pay.at[phase], phase + 1)

    def rowsums(*fields):
        v = jnp.concatenate([x[:, 0:128] + x[:, 128:256] for x in fields], axis=0)
        n = v.shape[0]
        r = dot(jnp.ones((8, 128), BF), jnp.concatenate(three(v), axis=0), NT)
        r = r[:, 0:n] + r[:, n:2 * n] + r[:, 2 * n:3 * n]
        parts = [r[0:1, loads * k:loads * k + loads] for k in range(len(fields))]
        return jnp.concatenate(parts + [jnp.zeros((1, loads), F32)] * (4 - len(fields)), axis=1)

    def through(rows, l):
        y = dot(rows, ptt[l])
        stack = doubled(folded(dot(y.astype(BF), s_buf[l])))
        for f in range(4):
            su[l, f] = folded(dot(stack, pt[l, f]))

    def jumped(z, x, l, f):
        if (l, f) == (0, 3):
            return z[3, 0] + z[2, 1]
        if (l, f) == (1, 2):
            return z[2, 1] + z[3, 0]
        return z[f, l] + x[f, l]

    stack = doubled(coarse(own_a, 0))
    modes0 = send_modes(stack, 0)
    copies0 = exchange(z0, x0, 0)
    for l in range(2):
        for f in range(4):
            sgb[l, :, width * f:width * f + width] = dot(ysb[l], pt[l, f]).astype(BF)
        for f in range(4):
            z0[f, l] = z0[f, l] - folded(dot(stack, sgb[l, :, width * f:width * f + width]))
        begin(copies0[3 * l:3 * l + 3])
    for l, f in both:
        mult[l, f] = folded(dot(stack, wlift[l, f]))
    own_b = sum_modes(modes0, 0, no_row)

    landing = [[n for n, side in enumerate(sides) if side[4] == l] for l in range(2)]
    t = jnp.zeros((128, 2 * loads), F32)
    for l, landed in enumerate(landing):
        finish([copies0[n] for n in landed], False)
        for f in range(4):
            r = jumped(z0, x0, l, f)
            res[l, f] = r
            rows[l, :, width * f:width * f + width] = doubled(r)
        t += dot(sgb[l], rows[l], NT)
    tzero[1] = squared(t)
    through(rows[0], 0)

    stack = doubled(coarse(own_b, 1))
    modes1 = send_modes(stack, 1)
    copies1 = exchange(z1, x1, 1)
    norm = jnp.zeros((32, width), F32)
    curve = jnp.zeros((32, width), F32)
    for l in range(2):
        if l == 1:
            through(rows[1], 1)
        for f in range(4):
            z = su[l, f] - folded(dot(stack, sgb[l, :, width * f:width * f + width]))
            z1[f, l] = z
            p = res[l, f] - folded(dot(stack, wlift[l, f]))
            d0[l, f] = p
            norm += p * p
            curve += p * z
        begin(copies1[3 * l:3 * l + 3])
    own_c = sum_modes(modes1, 1, rowsums(norm, 2.0 * curve))

    for l, landed in enumerate(landing):
        finish([copies1[n] for n in landed], False)
        for f in range(4):
            w = jumped(z1, x1, l, f)
            w0[l, f] = w
            rows[l, :, width * f:width * f + width] = doubled(w)
        through(rows[l], l)

    c = coarse(own_c, 2)
    stack = doubled(c)
    norm0 = c[:, 6:7]
    curve0 = c[:, 14:15]
    step0 = norm0 / curve0
    norm = jnp.zeros((32, width), F32)
    curve = jnp.zeros((32, width), F32)
    cross = jnp.zeros((32, width), F32)
    copies2 = exchange(z2, x2, 2)
    for l, f in both:
        p = d0[l, f] - step0 * (w0[l, f] - folded(dot(stack, wlift[l, f])))
        z = z1[f, l] - step0 * (su[l, f] - folded(dot(stack, sgb[l, :, width * f:width * f + width])))
        p1[l, f] = p
        z2[f, l] = z
        norm += p * p
        curve += p * z
        cross += p * z1[f, l]
    pay[2] = wide([jnp.zeros((3, 4 * loads), F32)], rowsums(norm, 2.0 * curve, 2.0 * cross))
    own_d = gather_start(pay.at[2], 3)
    begin(copies2)
    for l, f in both:
        mult[l, f] = mult[l, f] + step0 * d0[l, f]
        res[l, f] = res[l, f] - step0 * w0[l, f]
    finish(copies2, False)
    gather_finish(own_d, 3)
    total = jnp.sum(gath[3], axis=0)
    total = jnp.concatenate([total, jnp.zeros(total.shape, F32)], axis=0).T
    norm1, half1, cross1 = [total[loads * k:loads * k + loads, 3:4] for k in range(3)]
    beta = norm1 / norm0
    curve1 = half1 + 2.0 * beta * cross1 + beta * beta * curve0
    step1 = norm1 / curve1
    for l, f in both:
        mult_out[l, f] = mult[l, f] + step1 * (p1[l, f] + beta * d0[l, f])
        res_out[l, f] = res[l, f] - step1 * (jumped(z2, x2, l, f) + beta * w0[l, f])
    for group in (rcopies, kcopies, modes0, modes1, copies0, copies1, copies2):
        finish(group, True)
    for phase in range(4):
        many = gath.at[phase, pl.ds(0, n_dev - 1)]
        pltpu.make_async_copy(many, many, ag_send.at[phase]).wait()


def hand_over(mult, res, mult_out, res_out, sem):
    copies = [pltpu.make_async_copy(a, b, sem.at[n]) for n, (a, b) in enumerate(((mult, mult_out), (res, res_out)))]
    for c in copies:
        c.start()
    for c in copies:
        c.wait()


def local(n_sub, n_grp, schur, free, traces, load, coarse_inverse, face_map):
    n_dev = n_sub * n_grp
    loads, unk = free.shape[1], free.shape[2]
    width = face_map.shape[2]
    nr = 4 * n_dev
    vm = pl.BlockSpec(memory_space=pltpu.VMEM)
    hbm = pl.BlockSpec(memory_space=pl.ANY)
    field = pltpu.VMEM((2, 4, loads, width), F32)
    face = pltpu.VMEM((4, 2, loads, width), F32)
    dma = pltpu.SemaphoreType.DMA
    out = jax.ShapeDtypeStruct((2, 4, loads, width), F32)
    held = pltpu.VMEM((2, 4, loads, width), F32)
    results = pl.pallas_call(
        functools.partial(kernel, n_sub, n_grp),
        out_shape=(held, held),
        in_specs=[hbm] * 6,
        out_specs=(vm, vm),
        scratch_shapes=[
            pltpu.VMEM(free.shape, F32),
            pltpu.VMEM((traces.shape[1], 2, unk), F32),
            pltpu.VMEM((load.shape[1], 2, loads), F32),
            pltpu.VMEM(coarse_inverse.shape, F32),
            pltpu.VMEM(face_map.shape, jnp.int32),
            pltpu.VMEM((2, unk, unk), BF),
            pltpu.VMEM((2, 4, unk, width), BF),
            pltpu.VMEM((2, 4 * width, unk), BF),
            pltpu.VMEM((2, 128, unk), BF),
            pltpu.VMEM((2, 128, unk), BF),
            pltpu.VMEM((2, 128, 4 * width), BF),
            pltpu.VMEM((2, 2 * loads, 4 * width), BF),
            pltpu.VMEM((4, 2, 8, width), F32),
            pltpu.VMEM((4, 2, 8, width), F32),
            pltpu.VMEM((4, 16, nr), F32),
            pltpu.VMEM((4, 4, 16, nr), F32),
            pltpu.VMEM((256, 4 * nr), BF),
            pltpu.VMEM((2, 4, 64, width), F32),
            pltpu.VMEM((2, 4, 128, width), BF),
            pltpu.VMEM((128, 128), BF),
            pltpu.VMEM((64, loads), F32),
            pltpu.VMEM((2, 64, loads), F32),
            pltpu.VMEM((2, 5, 4, 4 * loads), F32),
            pltpu.VMEM((2, 4, 4, 4 * loads), F32),
            field, field, field, field, field, field,
            face, face, face, face, face, face,
            pltpu.VMEM((4, 4 * loads), F32),
            pltpu.VMEM((3, 4, 4 * loads), F32),
            pltpu.VMEM((4, n_dev, 4, 4 * loads), F32),
            dma, dma((5,)), dma((4,)), dma((4,)), dma((4,)), dma((4, 6)), dma((4, 6)), dma((4,)), dma((4,)),
            dma((2, 4)), dma((2, 4)),
        ],
        compiler_params=pltpu.CompilerParams(
            collective_id=0, has_side_effects=True, vmem_limit_bytes=56 * 1024 * 1024),
    )(schur, free, traces.transpose(1, 0, 2), load.transpose(1, 0, 2), coarse_inverse, face_map)
    return pl.pallas_call(
        hand_over, out_shape=(out, out), in_specs=[vm] * 2, out_specs=(hbm, hbm),
        scratch_shapes=[dma((2,))],
        compiler_params=pltpu.CompilerParams(vmem_limit_bytes=8 * 1024 * 1024))(*results)


def solution(mesh):
    both = ("sub", "grp")
    three_d = P(both, None, None)
    out = P(both, None, None, None)
    return jax.shard_map(
        functools.partial(local, mesh.shape["sub"], mesh.shape["grp"]), mesh=mesh,
        in_specs=(three_d, three_d, three_d, three_d, P(both, None), three_d),
        out_specs=(out, out), check_vma=False)
```
